32 devices in a mesh: groups: 2 (over x), radius: 16 (over z, y, core).
Axes of the slice: x: 2, y: 2, z: 4, core: 2. Of those that a mesh axis runs over, the one named last changes fastest.
Arguments:
- states: float32 [8, 400, 2048], P('groups', None, 'radius'), parts along dimension 0, may hold values from -6 to 6
- dipole: float32 [400, 400], replicated, may hold values from -0.625 to 0.625
- pattern: int32 [25, 25], replicated, may hold values 0 or 1
- angular: int32 [400], replicated, may hold values from 0 to 11
- thresholds: float32 [400], replicated, may hold values from 0 to 2
- surface_profile: float32 [2, 2048], P(None, 'radius'), may hold values from 0.2 to 1.5
- pulse_field: float32 [4], P('groups'), parts along dimension 0, may hold values from -0.05 to 0.05
Outputs:
- final_states: float32 [8, 400, 2048], P('groups', None, 'radius'), parts along dimension 0
- gradient: float32 [4], P('groups'), parts along dimension 0
The draws below stay inside these ranges and needn't reach their ends.
There are 2 independent parts, one for each index of `groups`. The reference program is written for one: setup_inputs(seed, part) draws one part's arguments, and reference() takes and returns one part's arrays. A program takes and returns all parts, laid end to end along the dimension named above; an argument that names none is the same for every part. Nothing has to cross between parts.
All inputs are finite; a program needn't handle non-finite values.
Results may differ from the reference program's by a relative error of at most 0.00019.
Values sent between devices are 32-bit elements; how exact they have to be, the bound alone decides.
No kernel may reach another device: no remote copies, remote signals or barrier semaphores. Data moves between devices by JAX's collectives and lax.ppermute only.
A program may use at most 64 MiB of HBM per device.

```python
import math
import jax
import jax.numpy as jnp
from jax import lax

C = 400
NBLK = 25
NR = 2048
STEPS = 2
ORDER = 4


def plant(drawn, stream_key, smallest, top_value):
    extent = drawn.shape
    place = [jax.random.randint(jax.random.fold_in(stream_key, axis), (), 0, extent[axis]) for axis in range(len(extent))]
    drawn = drawn.at[tuple(place)].set(smallest)
    longest = extent.index(max(extent))
    place[longest] = (place[longest] + 1) % extent[longest]
    return drawn.at[tuple(place)].set(top_value)


def levels(key, extent, split, least, largest):
    def one(dim, parts):
        heights = jax.random.uniform(jax.random.fold_in(jax.random.fold_in(key, 6), dim), (parts,), jnp.float32, least / len(split), largest / len(split))
        return jnp.repeat(jnp.exp(heights), extent[dim] // parts).reshape((-1,) + (1,) * (len(extent) - dim - 1))

    gain = one(*split[0])
    for cut in split[1:]:
        gain = gain * one(*cut)
    return gain


def scatter_about(rng, shape, width, reach, cuts=(), kind=jnp.bfloat16):
    values = jax.random.normal(rng, shape, jnp.float32) * width
    if len(cuts) > 0:
        values = levels(rng, shape, cuts, -0.22, 0.18) * values
    return jnp.clip(values, min=-reach, max=reach).astype(kind)


def setup_inputs(seed: int = 0, part: int = 0) -> dict:
    key_list = jax.random.split(jax.random.key(seed), 8)
    own_keys = jax.random.split(jax.random.fold_in(key_list[7], part), 8)
    states = scatter_about(own_keys[0], (4, C, NR), 1.0, 6.0, ((2, 16),), jnp.float32)
    dipole = scatter_about(key_list[1], (C, C), (C // 4) ** -0.5, 0.625, (), jnp.float32)
    pattern = plant((jax.random.randint(key_list[2], (NBLK, NBLK), 0, 2) < 1).astype(jnp.int32), jax.random.fold_in(key_list[2], 1), 0, 1)
    angular = plant(jax.random.randint(key_list[3], (C,), 0, 12), jax.random.fold_in(key_list[3], 1), 0, 11).astype(jnp.int32)
    thresholds = jnp.clip(jax.random.uniform(key_list[4], (C,), jnp.float32, 0.0, 2.0), 0.0, 2.0)
    surface_profile = jnp.clip(0.2 + 1.3 * jax.random.uniform(key_list[5], (2, NR), jnp.float32) ** levels(key_list[5], (2, NR), ((1, 16),), -0.2, 0.2), 0.2, 1.5)
    pulse_field = jnp.clip(jax.random.uniform(own_keys[6], (STEPS,), jnp.float32, -0.05, 0.05), -0.05, 0.05)
    return {"states": states, "dipole": dipole, "pattern": pattern, "angular": angular, "thresholds": thresholds, "surface_profile": surface_profile, "pulse_field": pulse_field}


inner_radius = 20.0
spacing = 0.08
time_step = 0.005

def coupling_matrix(dipole, pattern, angular):
    channels = dipole.shape[0]
    blocks = pattern.shape[0]
    block_size = channels // blocks
    joined = jnp.maximum(pattern, pattern.T)
    block_owner = jnp.arange(channels, dtype=jnp.int32) // block_size
    block_pick = (block_owner[:, None] == jnp.arange(blocks, dtype=jnp.int32)[None, :]).astype(jnp.int32)
    block_mask = jnp.dot(jnp.dot(block_pick, joined), block_pick.T)
    selection = jnp.abs(angular[:, None] - angular[None, :]) == 1
    allowed = (block_mask > 0) & selection
    return jnp.where(allowed, 0.5 * (dipole + dipole.T), jnp.zeros_like(dipole))

def surface_pair(points):
    value_row = 4.0 * points[:, :, 0] - 6.0 * points[:, :, 1] + 4.0 * points[:, :, 2] - points[:, :, 3]
    slope_row = -13.0 / 3.0 * points[:, :, 0] + 9.5 * points[:, :, 1] - 7.0 * points[:, :, 2] + 11.0 / 6.0 * points[:, :, 3]
    return jnp.stack([value_row, slope_row])

def apply_hamiltonian(extended, positions, profile_rows, boundary, coupling, thresholds, centrifugal, strength, power, grid_points):
    center = extended[:, :, 2:-2]
    radial_values = inner_radius + (positions + 1).astype(jnp.float32) * spacing
    kinetic = -0.5 / (spacing * spacing) * (-1.0 / 12.0 * (extended[:, :, :-4] + extended[:, :, 4:]) + 4.0 / 3.0 * (extended[:, :, 1:-3] + extended[:, :, 3:-1]) - 2.5 * center)
    potential = (thresholds[:, None] + centrifugal[:, None] / (radial_values * radial_values)[None, :]) * center
    mixed_rows = jnp.einsum('cd,kdr->kcr', coupling, center, precision=lax.Precision.HIGHEST)
    driven = (strength * radial_values)[None, None, :] * mixed_rows
    boundary_term = boundary[0][:, :, None] * profile_rows[0][None, None, :] + boundary[1][:, :, None] * profile_rows[1][None, None, :]
    hamiltonian = kinetic + potential + driven + boundary_term
    advanced = time_step / power * jnp.stack([hamiltonian[1], -hamiltonian[0], hamiltonian[3], -hamiltonian[2]])
    inside = (positions >= 0) & (positions < grid_points)
    return (jnp.where(inside[None, None, :], advanced, jnp.zeros_like(advanced)), mixed_rows)

def reference(states, dipole, pattern, angular, thresholds, surface_profile, pulse_field):
    coupling = coupling_matrix(dipole, pattern, angular)
    centrifugal = 0.5 * (angular * (angular + 1)).astype(jnp.float32)
    positions = jnp.arange(NR, dtype=jnp.int32)
    radial_values = inner_radius + (positions + 1).astype(jnp.float32) * spacing
    normalizer = math.sqrt(C * NR) * (inner_radius + NR * spacing)
    intersections = []
    for step_index in range(STEPS):
        strength = pulse_field[step_index]
        summed = states
        taylor_term = states
        for power in range(1, ORDER + 1):
            boundary = surface_pair(taylor_term[:, :, :4])
            extended = jnp.pad(taylor_term, ((0, 0), (0, 0), (2, 2)))
            taylor_term, mixed_rows = apply_hamiltonian(extended, positions, surface_profile, boundary, coupling, thresholds, centrifugal, strength, power, NR)
            if power == 1:
                intersection = jnp.sum(radial_values[None, :] * (states[2] * mixed_rows[1] - states[3] * mixed_rows[0]))
                intersections.append(intersection)
            summed = summed + taylor_term
        states = summed
    return (states, jnp.stack(intersections) / normalizer)
```

```python
import functools
import math

import jax
import jax.numpy as jnp
from jax import lax
from jax.experimental import pallas as pl
from jax.experimental.pallas import tpu as pltpu
from jax.sharding import PartitionSpec as P

STEPS = 2
ORDER = 4

inner_radius = 20.0
spacing = 0.08
time_step = 0.005

HALO = 2 * ORDER * STEPS
INNER = 24
KIN = 1.0 / (24.0 * spacing * spacing)
VALUE = (4.0, -6.0, 4.0, -1.0)
SLOPE = (-13.0 / 3.0, 9.5, -7.0, 11.0 / 6.0)

F32 = jnp.float32
BF16 = jnp.bfloat16

OWN = {"a": 0, "c": 128, "b": 512, "d": 640}
EXTRA = {"a": 256, "c": 256, "b": 384, "d": 384}
PARTS = ("a", "b", "c", "d")


def iota(shape, dim):
    return lax.broadcasted_iota(jnp.int32, shape, dim)


def pack_kernel(states_ref, profile_ref, right_ref, left_ref, inner_ref):
    channels = states_ref.shape[1]
    half = channels // 2
    local = states_ref.shape[2]

    def gather(rows_ref, rows, moves, lanes):
        out = None
        for part, source, target, width in moves:
            moved = rows_ref[part, rows, :]
            shift = (target - source) % local
            if shift:
                moved = pltpu.roll(moved, shift, 1)
            if out is None:
                out = moved
            else:
                inside = (lanes >= target) & (lanes < target + width)
                out = jnp.where(inside, moved, out)
        return out

    order = {0: 0, 2: 64, 1: 16, 3: 80}
    lanes = iota((half, local), 1)
    right = None
    for out_ref, source in ((right_ref, local - HALO), (left_ref, 0)):
        packed = None
        for h in range(2):
            moves = [(k, source, order[k] + 32 * h, HALO) for k in range(4)]
            got = gather(states_ref, pl.ds(half * h, half), moves, lanes)
            if packed is None:
                packed = got
            else:
                packed = jnp.where((lanes & 32) != 0, got, packed)
        out_ref[:half, :] = packed
        prof = profile_ref[...]
        shift = (-source) % local
        if shift:
            prof = pltpu.roll(prof, shift, 1)
        out_ref[half : half + 2, :] = prof
        out_ref[half + 2 :, :] = jnp.zeros((out_ref.shape[0] - half - 2, local), F32)

    lanes = iota((channels, local), 1)
    moves = []
    for k, first in ((0, 32), (2, 96), (1, 0), (3, 64)):
        moves.append((k, 0, first, INNER))
        moves.append((k, 0, first + INNER, 8))
    inner_ref[:channels, :] = gather(states_ref, pl.ds(0, channels), moves, lanes)
    prof = profile_ref[...]
    lanes2 = iota((2, local), 1)
    shifted = pltpu.roll(prof, 32, 1)
    inner_ref[channels : channels + 2, :] = jnp.where(
        (lanes2 & 63) >= 32 + INNER, pltpu.roll(prof, 32 + INNER, 1), shifted
    )
    inner_ref[channels + 2 :, :] = jnp.zeros((inner_ref.shape[0] - channels - 2, local), F32)


def lane_points(lanes, first, local):
    e = (lanes - local) & 63
    own = lanes < local
    point = jnp.where(
        own,
        first + lanes,
        jnp.where(
            e < 16,
            first - 16 + e,
            jnp.where(
                e < 32,
                first + local + e - 16,
                jnp.where(e < 32 + INNER, e - 32, e - 32 - INNER),
            ),
        ),
    )
    segment = jnp.where(own, 0, jnp.where(e < 32, 0, jnp.where(e < 32 + INNER, 1, 2)))
    return point, segment


def table_kernel(
    first_ref, dipole_ref, pattern_ref, angular_ref, thr_ref, coupling_ref, kinetic_ref, pot_ref, *, grid_points
):
    channels = dipole_ref.shape[0]
    blocks = pattern_ref.shape[0]
    size = channels // blocks
    local = 128
    first = first_ref[0]
    pattern = pattern_ref[...].astype(F32)
    joined = jnp.maximum(pattern, pattern.T).astype(BF16)
    tall = (iota((channels, blocks), 0) // size == iota((channels, blocks), 1)).astype(F32).astype(BF16)
    wide = (iota((blocks, channels), 1) // size == iota((blocks, channels), 0)).astype(F32).astype(BF16)
    rows = jnp.dot(tall, joined, preferred_element_type=F32).astype(BF16)
    mask = jnp.dot(rows, wide, preferred_element_type=F32)
    ang = jnp.broadcast_to(angular_ref[...].astype(F32), (channels, channels))
    angt = ang.T
    allowed = (mask > 0.5) & (jnp.abs(ang - angt) == 1.0)
    dip = dipole_ref[...]
    coupling = jnp.where(allowed, 0.5 * (dip + dip.T), 0.0)
    high = coupling.astype(BF16)
    low = (coupling - high.astype(F32)).astype(BF16)
    coupling_ref[...] = jnp.concatenate([high, high, low], axis=1)
    lanes = iota((8, 2 * local), 1)
    point, _ = lane_points(lanes, first, local)
    radii = inner_radius + (point + 1).astype(F32) * spacing
    inverse = (1.0 / (radii * radii))[:1]
    centrifugal = 0.5 * angt[:, :local] * (angt[:, :local] + 1.0)
    thr = jnp.broadcast_to(thr_ref[...], (local, channels)).T
    pot_ref[:, :local] = thr + centrifugal * inverse[:, :local]
    pot_ref[:, local:] = thr + centrifugal * inverse[:, local:]
    shape = (2 * local, 2 * local)
    src, dst = iota(shape, 0), iota(shape, 1)
    sp, ss = lane_points(src, first, local)
    dp, ds = lane_points(dst, first, local)
    gap = jnp.abs(sp - dp)
    coef = jnp.where(gap == 0, 30.0, jnp.where(gap == 1, -16.0, jnp.where(gap == 2, 1.0, 0.0)))
    same = (ss < 2) & (ss == jnp.minimum(ds, 1))
    valid = (dp >= 0) & (dp < grid_points) & ((dst < local) | (((dst - local) & 63) < 60))
    coef = jnp.where(same & valid, coef, 0.0)
    for which in range(2):
        mine = (src < local) | ((src - local) // 64 == which)
        mine = mine & ((dst < local) | ((dst - local) // 64 == which))
        kinetic_ref[which] = jnp.where(mine, coef, 0.0)


def split_store(stack_ref, at, value):
    channels = value.shape[0]
    width = value.shape[1]
    high = value.astype(BF16)
    low = (value - high.astype(F32)).astype(BF16)
    stack_ref[:channels, at : at + width] = high
    stack_ref[channels : 2 * channels, at : at + width] = low
    stack_ref[2 * channels :, at : at + width] = high


def lane_radii(first, local):
    lanes = iota((8, 2 * local), 1)
    point, _ = lane_points(lanes, first, local)
    return (inner_radius + (point + 1).astype(F32) * spacing)[:1]


def mix(coupling_ref, stack_ref, mixed_ref):
    for n in range(3):
        cut = slice(256 * n, 256 * n + 256)
        mixed_ref[:, cut] = jnp.dot(coupling_ref[...], stack_ref[:, cut], preferred_element_type=F32)


def stencil(stack_ref, matrix_ref, moved_ref):
    channels = stack_ref.shape[0] // 3
    for k, part in enumerate(PARTS):
        own, extra = OWN[part], EXTRA[part]
        weights = matrix_ref[0 if part in "ab" else 1]
        total = None
        for rows in (slice(0, channels), slice(channels, 2 * channels)):
            left = jnp.concatenate([stack_ref[rows, own : own + 128], stack_ref[rows, extra : extra + 128]], axis=1)
            got = jnp.dot(left, weights, preferred_element_type=F32)
            total = got if total is None else total + got
        moved_ref[k] = total


def advance(v_ref, total_ref, stack_ref, mixed_ref, moved_ref, pot_ref, drive, scale, chunk=80):
    channels = v_ref.shape[0]
    local = 128
    for c0 in range(0, channels, chunk):
        rows = slice(c0, c0 + chunk)
        pot_own, pot_extra = pot_ref[rows, :local], pot_ref[rows, local:]
        drive_own, drive_extra = drive[:, :local], drive[:, local:]

        def hamiltonian(at, moved, pot, force):
            cut = slice(at, at + local)
            return KIN * moved + pot * v_ref[rows, cut] + force * mixed_ref[rows, cut]

        new = {}
        for source, target, sign in ((1, "a", 1.0), (0, "b", -1.0), (3, "c", 1.0), (2, "d", -1.0)):
            part = PARTS[source]
            new[OWN[target]] = (sign * scale) * hamiltonian(
                OWN[part], moved_ref[source, rows, :local], pot_own, drive_own
            )
        for source, target, sign in (("b", "a", 1.0), ("a", "b", -1.0)):
            k = PARTS.index(source)
            moved = moved_ref[k, rows, local:] + moved_ref[k + 2, rows, local:]
            new[EXTRA[target]] = (sign * scale) * hamiltonian(EXTRA[source], moved, pot_extra, drive_extra)
        for at, value in new.items():
            cut = slice(at, at + local)
            v_ref[rows, cut] = value
            total_ref[rows, cut] = total_ref[rows, cut] + value
            high = value.astype(BF16)
            low = (value - high.astype(F32)).astype(BF16)
            stack_ref[c0 : c0 + chunk, cut] = high
            stack_ref[channels + c0 : channels + c0 + chunk, cut] = low
            stack_ref[2 * channels + c0 : 2 * channels + c0 + chunk, cut] = high


def intersect(state_ref, mixed_ref, radii):
    def at(ref, part):
        return ref[:, OWN[part] : OWN[part] + 128]

    both = at(state_ref, "c") * at(mixed_ref, "b") - at(state_ref, "d") * at(mixed_ref, "a")
    return jnp.sum(both * radii[:, :128], axis=0, keepdims=True)


def first_kernel(
    first_ref,
    field_ref,
    states_ref,
    left_ref,
    right_ref,
    inner_ref,
    profile_ref,
    coupling_ref,
    kinetic_ref,
    pot_ref,
    state_ref,
    mixed_ref,
    matrix_ref,
    part_ref,
    v_ref,
    stack_ref,
    moved_ref,
    work_ref,
):
    channels = states_ref.shape[1]
    half = channels // 2
    local = 128
    first = first_ref[0]
    for k, part in enumerate(PARTS):
        v_ref[:, OWN[part] : OWN[part] + local] = states_ref[k]
    lanes = iota((half, local), 1) & 63
    for pair, at in ((0, 256), (1, 384)):
        for h in range(2):
            rows = slice(half * h, half * h + half)
            back = 16 * pair + 32 * h
            lo = left_ref[:half, :]
            ro = right_ref[:half, :]
            if back:
                lo = pltpu.roll(lo, local - back, 1)
            if back != 16:
                ro = pltpu.roll(ro, (16 - back) % local, 1)
            io = inner_ref[rows, :]
            if pair:
                io = pltpu.roll(io, 32, 1)
            v_ref[rows, at : at + local] = jnp.where(lanes < 16, lo, jnp.where(lanes < 32, ro, io))
    state_ref[...] = v_ref[...]
    split_store(stack_ref, 0, v_ref[...])
    p_own = profile_ref[...]
    lanes2 = iota((2, local), 1)
    p_extra = jnp.where(
        lanes2 < 16,
        left_ref[half : half + 2, :],
        jnp.where(lanes2 < 32, pltpu.roll(right_ref[half : half + 2, :], 16, 1), inner_ref[channels : channels + 2, :]),
    )
    p_extra = jnp.where((lanes2 & 63) < 60, p_extra, 0.0)
    p_extra = jnp.where(lanes2 < 64, p_extra, pltpu.roll(p_extra, 64, 1))
    profile = jnp.concatenate([p_own, p_extra], axis=1)
    cols = iota((1, 2 * local), 1)
    work_ref[...] = kinetic_ref[...]
    for which in range(2):
        mine = (cols < local) | ((cols - local) // 64 == which)
        for i in range(4):
            row = (VALUE[i] / KIN) * profile[0:1] + (SLOPE[i] / KIN) * profile[1:2]
            at = local + 64 * which + 32 + i
            row = jnp.where(mine, row, 0.0) + work_ref[which, at : at + 1, :]
            high = row.astype(BF16).astype(F32)
            work_ref[which, at : at + 1, :] = high
            at = local + 64 * which + 32 + INNER + i
            work_ref[which, at : at + 1, :] = row - high
    matrix_ref[...] = work_ref[...].astype(BF16)
    radii = lane_radii(first, local)
    drive = field_ref[0] * radii
    for power in range(1, ORDER + 1):
        mix(coupling_ref, stack_ref, mixed_ref)
        stencil(stack_ref, matrix_ref, moved_ref)
        if power == 1:
            part_ref[0:1, :] = intersect(state_ref, mixed_ref, radii)
        advance(v_ref, state_ref, stack_ref, mixed_ref, moved_ref, pot_ref, drive, time_step / power)
    split_store(stack_ref, 0, state_ref[...])
    mix(coupling_ref, stack_ref, mixed_ref)
    part_ref[1:2, :] = intersect(state_ref, mixed_ref, radii)
    part_ref[2:, :] = jnp.zeros((part_ref.shape[0] - 2, local), F32)


def second_kernel(
    first_ref, field_ref, state_in_ref, mixed_in_ref, matrix_ref, coupling_ref, pot_ref, out_ref, v_ref, total_ref, stack_ref, mixed_ref, moved_ref
):
    local = 128
    radii = lane_radii(first_ref[0], local)
    drive = field_ref[1] * radii
    v_ref[...] = state_in_ref[...]
    total_ref[...] = state_in_ref[...]
    split_store(stack_ref, 0, state_in_ref[...])
    for power in range(1, ORDER + 1):
        if power > 1:
            mix(coupling_ref, stack_ref, mixed_ref)
        stencil(stack_ref, matrix_ref, moved_ref)
        advance(
            v_ref,
            total_ref,
            stack_ref,
            mixed_in_ref if power == 1 else mixed_ref,
            moved_ref,
            pot_ref,
            drive,
            time_step / power,
        )
    for k, part in enumerate(PARTS):
        out_ref[k] = total_ref[:, OWN[part] : OWN[part] + local]


def tree(count):
    if count == 16:
        return [[2], [4, 8, 12], [1]]
    return [[1 << k] for k in range((count - 1).bit_length())]


def broadcast(value, axis, count):
    here = lax.axis_index(axis)
    have = [0]
    for offsets in tree(count):
        fresh, chosen = [], value
        for offset in offsets:
            pairs = [(h, h + offset) for h in have if h + offset < count]
            got = lax.ppermute(value, axis, pairs)
            to = [p[1] for p in pairs]
            hit = functools.reduce(jnp.logical_or, [here == t for t in to])
            chosen = jnp.where(hit, got, chosen)
            fresh += to
        value = chosen
        have += fresh
    return value


def vmem(count):
    return [pl.BlockSpec(memory_space=pltpu.VMEM)] * count


def smem(count):
    return [pl.BlockSpec(memory_space=pltpu.SMEM)] * count


def params():
    return pltpu.CompilerParams(vmem_limit_bytes=48 * 1024 * 1024)


def per_device(states, dipole, pattern, angular, thresholds, surface_profile, pulse_field, *, count):
    channels, local = states.shape[1:]
    grid_points = local * count
    half = channels // 2
    axis = "radius"
    first = (lax.axis_index(axis) * local).reshape(1).astype(jnp.int32)
    shape = jax.ShapeDtypeStruct

    to_right, to_left, inner = pl.pallas_call(
        pack_kernel,
        out_shape=(shape((half + 8, local), F32), shape((half + 8, local), F32), shape((channels + 8, local), F32)),
        in_specs=vmem(2),
        out_specs=tuple(vmem(3)),
        compiler_params=params(),
        name="pack",
    )(states, surface_profile)
    left = lax.ppermute(to_right, axis, [(i, i + 1) for i in range(count - 1)])
    right = lax.ppermute(to_left, axis, [(i + 1, i) for i in range(count - 1)])
    inner = broadcast(inner, axis, count)

    coupling, kinetic, pot = pl.pallas_call(
        functools.partial(table_kernel, grid_points=grid_points),
        out_shape=(
            shape((channels, 3 * channels), BF16),
            shape((2, 2 * local, 2 * local), F32),
            shape((channels, 2 * local), F32),
        ),
        in_specs=smem(1) + vmem(4),
        out_specs=tuple(vmem(3)),
        compiler_params=params(),
        name="tables",
    )(first, dipole, pattern, angular.reshape(1, channels), thresholds.reshape(1, channels))

    width = 6 * local
    state, mixed, matrix, part = pl.pallas_call(
        first_kernel,
        out_shape=(
            shape((channels, width), F32),
            shape((channels, width), F32),
            shape((2, 2 * local, 2 * local), BF16),
            shape((8, local), F32),
        ),
        in_specs=smem(2) + vmem(8),
        out_specs=tuple(vmem(4)),
        scratch_shapes=[
            pltpu.VMEM((channels, width), F32),
            pltpu.VMEM((3 * channels, width), BF16),
            pltpu.VMEM((4, channels, 2 * local), F32),
            pltpu.VMEM((2, 2 * local, 2 * local), F32),
        ],
        compiler_params=params(),
        name="first",
    )(first, pulse_field, states, left, right, inner, surface_profile, coupling, kinetic, pot)

    final = pl.pallas_call(
        second_kernel,
        out_shape=shape(states.shape, F32),
        in_specs=smem(2) + vmem(5),
        out_specs=vmem(1)[0],
        scratch_shapes=[
            pltpu.VMEM((channels, width), F32),
            pltpu.VMEM((channels, width), F32),
            pltpu.VMEM((3 * channels, width), BF16),
            pltpu.VMEM((channels, width), F32),
            pltpu.VMEM((4, channels, 2 * local), F32),
        ],
        compiler_params=params(),
        name="second",
    )(first, pulse_field, state, mixed, matrix, coupling, pot)

    bit = 1
    while bit < count:
        part = part + lax.ppermute(part, axis, [(i, i ^ bit) for i in range(count)])
        bit *= 2
    normalizer = math.sqrt(channels * grid_points) * (inner_radius + grid_points * spacing)
    gradient = jnp.sum(part[:STEPS], axis=1) / normalizer
    return final, gradient


def solution(mesh):
    return jax.shard_map(
        functools.partial(per_device, count=mesh.shape["radius"]),
        mesh=mesh,
        in_specs=(P("groups", None, "radius"), P(), P(), P(), P(), P(None, "radius"), P("groups")),
        out_specs=(P("groups", None, "radius"), P("groups")),
        check_vma=False,
    )
```

```python
import functools
import math

import jax
import jax.numpy as jnp
from jax import lax
from jax.experimental import pallas as pl
from jax.experimental.pallas import tpu as pltpu
from jax.sharding import PartitionSpec as P

STEPS = 2
ORDER = 4

inner_radius = 20.0
spacing = 0.08
time_step = 0.005

HALO = 2 * ORDER * STEPS
INNER = 2 * ORDER * STEPS + 2
KIN = 1.0 / (24.0 * spacing * spacing)
VALUE = (4.0, -6.0, 4.0, -1.0)
SLOPE = (-13.0 / 3.0, 9.5, -7.0, 11.0 / 6.0)

F32 = jnp.float32
BF16 = jnp.bfloat16

OWN = {"a": 0, "c": 128, "b": 512, "d": 640}
EXTRA = {"a": 256, "c": 256, "b": 384, "d": 384}
PARTS = ("a", "b", "c", "d")


def iota(shape, dim):
    return lax.broadcasted_iota(jnp.int32, shape, dim)


def is_odd(first, local):
    return lax.rem(lax.div(first, local), 2) == 1


def pack_kernel(first_ref, states_any, profile_any, near_ref, far_ref, inner_ref, states_ref, profile_ref, sems):
    channels = states_ref.shape[1]
    half = channels // 2
    local = states_ref.shape[2]
    copies = [pltpu.make_async_copy(states_any.at[k], states_ref.at[k], sems.at[k]) for k in range(4)]
    copies.append(pltpu.make_async_copy(profile_any, profile_ref, sems.at[4]))
    for copy in copies:
        copy.start()
    copies[4].wait()
    odd = is_odd(first_ref[0], local)
    zeros = jnp.zeros((6, local), F32)
    prof = profile_ref[...]
    turned = pltpu.roll(prof, HALO, 1)
    for ref, value in (
        (near_ref, jnp.where(odd, prof, turned)),
        (far_ref, jnp.where(odd, turned, prof)),
        (inner_ref, prof),
    ):
        ref[half : half + 2, :] = value
        ref[half + 2 : half + 8, :] = zeros
    group = iota((half, local), 1) // 16
    pair = (iota((channels, local), 1) & 63) // 2
    right = left = more = None
    for k, first in ((0, 0), (2, 64), (1, 16), (3, 80)):
        copies[k].wait()
        for h in range(2):
            rows = states_ref[k, half * h : half * h + half, :]
            at = first + 32 * h
            hit = group == at // 16
            shift = (at + HALO) % local
            moved = pltpu.roll(rows, shift, 1) if shift else rows
            right = moved if right is None else jnp.where(hit, moved, right)
            moved = pltpu.roll(rows, at, 1) if at else rows
            left = moved if left is None else jnp.where(hit, moved, left)
        at = 64 * (k // 2) + 2 * (k % 2)
        moved = pltpu.roll(states_ref[k], (at - 16) % local, 1)
        more = moved if more is None else jnp.where(pair == k % 2, jnp.where(iota((channels, local), 1) // 64 == k // 2, moved, more), more)
    near_ref[:half, :] = jnp.where(odd, left, right)
    far_ref[:half, :] = jnp.where(odd, right, left)
    inner_ref[:half, :] = left
    rest = None
    quad = (iota((32, local), 1) & 63) // 4
    for i in range((channels + 31) // 32):
        rows = more[32 * i : min(32 * i + 32, channels)]
        if rows.shape[0] < 32:
            rows = jnp.concatenate([rows, jnp.zeros((32 - rows.shape[0], local), F32)], axis=0)
        moved = pltpu.roll(rows, 4 * i, 1) if i else rows
        rest = moved if rest is None else jnp.where(quad == i, moved, rest)
    inner_ref[half + 8 :, :] = rest


def lane_points(lanes, first, local):
    e = (lanes - local) & 63
    own = lanes < local
    point = jnp.where(
        own,
        first + lanes,
        jnp.where(
            e < 16,
            first - 16 + e,
            jnp.where(
                e < 32,
                first + local + e - 16,
                jnp.where(e < 32 + INNER, e - 32, e - 32 - INNER),
            ),
        ),
    )
    segment = jnp.where(
        own, 0, jnp.where(e < 32, 0, jnp.where(e < 32 + INNER, 1, jnp.where(e < 36 + INNER, 2, 3)))
    )
    return point, segment


def lane_radii(first, local):
    lanes = iota((8, 2 * local), 1)
    point, _ = lane_points(lanes, first, local)
    return (inner_radius + (point + 1).astype(F32) * spacing)[:1]


def table_kernel(
    first_ref,
    dipole_ref,
    pattern_ref,
    angular_ref,
    thr_ref,
    states_ref,
    coupling_ref,
    kinetic_ref,
    pot_ref,
    v_ref,
    stack_ref,
    mixed_ref,
    part_ref,
    *,
    grid_points,
):
    channels = dipole_ref.shape[0]
    blocks = pattern_ref.shape[0]
    size = channels // blocks
    local = 128
    first = first_ref[0]
    pattern = pattern_ref[...].astype(F32)
    joined = jnp.maximum(pattern, pattern.T).astype(BF16)
    tall = (iota((channels, blocks), 0) // size == iota((channels, blocks), 1)).astype(F32).astype(BF16)
    wide = (iota((blocks, channels), 1) // size == iota((blocks, channels), 0)).astype(F32).astype(BF16)
    rows = jnp.dot(tall, joined, preferred_element_type=F32).astype(BF16)
    mask = jnp.dot(rows, wide, preferred_element_type=F32)
    ang = jnp.broadcast_to(angular_ref[...].astype(F32), (channels, channels))
    angt = ang.T
    allowed = (mask > 0.5) & (jnp.abs(ang - angt) == 1.0)
    dip = dipole_ref[...]
    coupling = jnp.where(allowed, 0.5 * (dip + dip.T), 0.0)
    high = coupling.astype(BF16)
    low = (coupling - high.astype(F32)).astype(BF16)
    coupling_ref[...] = jnp.concatenate([high, high, low], axis=1)
    radii = lane_radii(first, local)
    inverse = 1.0 / (radii * radii)
    centrifugal = 0.5 * angt[:, :local] * (angt[:, :local] + 1.0)
    thr = jnp.broadcast_to(thr_ref[...], (local, channels)).T
    pot_ref[:, :local] = thr + centrifugal * inverse[:, :local]
    pot_ref[:, local:] = thr + centrifugal * inverse[:, local:]
    shape = (2 * local, 2 * local)
    src, dst = iota(shape, 0), iota(shape, 1)
    sp, ss = lane_points(src, first, local)
    dp, ds = lane_points(dst, first, local)
    gap = jnp.abs(sp - dp)
    coef = jnp.where(gap == 0, 30.0, jnp.where(gap == 1, -16.0, jnp.where(gap == 2, 1.0, 0.0)))
    same = (ss < 2) & (ss == jnp.minimum(ds, 1))
    valid = (dp >= 0) & (dp < grid_points) & (ds < 3)
    coef = jnp.where(same & valid, coef, 0.0)
    for which in range(2):
        mine = (src < local) | ((src - local) // 64 == which)
        mine = mine & ((dst < local) | ((dst - local) // 64 == which))
        kinetic_ref[which] = jnp.where(mine, coef, 0.0)
    for k, part in enumerate(PARTS):
        at = OWN[part]
        v_ref[:, at : at + local] = states_ref[k]
        split_store(stack_ref, at, states_ref[k])
    mix(coupling_ref, stack_ref, mixed_ref, (0, 2))
    part_ref[0:1, :] = intersect(v_ref, mixed_ref, radii)
    part_ref[1:, :] = jnp.zeros((part_ref.shape[0] - 1, local), F32)


def split_store(stack_ref, at, value):
    channels = value.shape[0]
    width = value.shape[1]
    high = value.astype(BF16)
    low = (value - high.astype(F32)).astype(BF16)
    stack_ref[:channels, at : at + width] = high
    stack_ref[channels : 2 * channels, at : at + width] = low
    stack_ref[2 * channels :, at : at + width] = high


def mix(coupling_ref, stack_ref, mixed_ref, tiles):
    for n in tiles:
        cut = slice(256 * n, 256 * n + 256)
        mixed_ref[:, cut] = jnp.dot(coupling_ref[...], stack_ref[:, cut], preferred_element_type=F32)


def stencil(stack_ref, matrix_ref, moved_ref):
    channels = stack_ref.shape[0] // 3
    for k, part in enumerate(PARTS):
        own, extra = OWN[part], EXTRA[part]
        weights = matrix_ref[0 if part in "ab" else 1]
        total = None
        for rows in (slice(0, channels), slice(channels, 2 * channels)):
            left = jnp.concatenate([stack_ref[rows, own : own + 128], stack_ref[rows, extra : extra + 128]], axis=1)
            got = jnp.dot(left, weights, preferred_element_type=F32)
            total = got if total is None else total + got
        moved_ref[k] = total


def advance(v_ref, total_ref, stack_ref, mixed_ref, moved_ref, pot_ref, drive, scale, own_only=False, chunk=80):
    channels = v_ref.shape[0]
    local = 128
    for c0 in range(0, channels, chunk):
        rows = slice(c0, c0 + chunk)
        pot_own, pot_extra = pot_ref[rows, :local], pot_ref[rows, local:]
        drive_own, drive_extra = drive[:, :local], drive[:, local:]

        def hamiltonian(at, moved, pot, force):
            cut = slice(at, at + local)
            return KIN * moved + pot * v_ref[rows, cut] + force * mixed_ref[rows, cut]

        new = {}
        for source, target, sign in ((1, "a", 1.0), (0, "b", -1.0), (3, "c", 1.0), (2, "d", -1.0)):
            part = PARTS[source]
            new[OWN[target]] = (sign * scale) * hamiltonian(
                OWN[part], moved_ref[source, rows, :local], pot_own, drive_own
            )
        if not own_only:
            for source, target, sign in (("b", "a", 1.0), ("a", "b", -1.0)):
                k = PARTS.index(source)
                moved = moved_ref[k, rows, local:] + moved_ref[k + 2, rows, local:]
                new[EXTRA[target]] = (sign * scale) * hamiltonian(EXTRA[source], moved, pot_extra, drive_extra)
        for at, value in new.items():
            cut = slice(at, at + local)
            total_ref[rows, cut] = total_ref[rows, cut] + value
            if own_only:
                continue
            v_ref[rows, cut] = value
            high = value.astype(BF16)
            low = (value - high.astype(F32)).astype(BF16)
            stack_ref[c0 : c0 + chunk, cut] = high
            stack_ref[channels + c0 : channels + c0 + chunk, cut] = low
            stack_ref[2 * channels + c0 : 2 * channels + c0 + chunk, cut] = high


def intersect(state_ref, mixed_ref, radii):
    def at(ref, part):
        return ref[:, OWN[part] : OWN[part] + 128]

    both = at(state_ref, "c") * at(mixed_ref, "b") - at(state_ref, "d") * at(mixed_ref, "a")
    return jnp.sum(both * radii[:, :128], axis=0, keepdims=True)


def first_kernel(
    first_ref,
    field_ref,
    far_ref,
    got_ref,
    sent_ref,
    profile_ref,
    coupling_ref,
    kinetic_ref,
    pot_ref,
    part_in_ref,
    v_in_ref,
    stack_in_ref,
    mixed_in_ref,
    v_ref,
    stack_ref,
    mixed_ref,
    state_ref,
    matrix_ref,
    part_ref,
    moved_ref,
    work_ref,
    *,
    scaling,
):
    del v_in_ref, stack_in_ref, mixed_in_ref
    channels = v_ref.shape[0]
    half = channels // 2
    local = 128
    first = first_ref[0]
    odd = is_odd(first, local)
    split = half + 40
    inner = jnp.where(odd, got_ref[:split, :], sent_ref[:split, :])
    left = jnp.where(odd, got_ref[split:, :], far_ref[...])
    right = jnp.where(odd, far_ref[...], got_ref[split:, :])
    lanes = iota((half, local), 1) & 63
    for pair, at in ((0, 256), (1, 384)):
        for h in range(2):
            back = 16 * pair + 32 * h

            def rolled(value, to):
                shift = (to - back) % local
                return pltpu.roll(value, shift, 1) if shift else value

            value = jnp.where(
                lanes < 16,
                rolled(left[:half, :], 0),
                jnp.where(
                    lanes < 32,
                    rolled(right[:half, :], 16),
                    jnp.where(
                        lanes < 48,
                        rolled(inner[:half, :], 32),
                        jnp.where(
                            (lanes >= 50) & (lanes < 54), rolled(inner[:half, :], 50), jnp.zeros((half, local), F32)
                        ),
                    ),
                ),
            )
            v_ref[half * h : half * h + half, at : at + local] = value
        narrow = iota((32, local), 1) & 63
        for i in range((channels + 31) // 32):
            rows = slice(32 * i, min(32 * i + 32, channels))
            count = rows.stop - rows.start
            value = pltpu.roll(inner[half + 8 : half + 8 + count, :], (48 - 4 * i - 2 * pair) % local, 1)
            hit = (narrow[:count] >= 48) & (narrow[:count] < 50)
            v_ref[rows, at : at + local] = jnp.where(hit, value, v_ref[rows, at : at + local])
    state_ref[...] = v_ref[...]
    split_store(stack_ref, 256, v_ref[:, 256:512])
    p_own = profile_ref[...]
    lanes2 = iota((2, local), 1)
    inner_profile = inner[half : half + 2, :]
    p_extra = jnp.where(
        lanes2 < 16,
        left[half : half + 2, :],
        jnp.where(
            lanes2 < 32,
            pltpu.roll(right[half : half + 2, :], 16, 1),
            jnp.where(
                lanes2 < 32 + INNER,
                pltpu.roll(inner_profile, 32, 1),
                jnp.where(lanes2 < 36 + INNER, pltpu.roll(inner_profile, 32 + INNER, 1), 0.0),
            ),
        ),
    )
    p_extra = jnp.where(lanes2 < 64, p_extra, pltpu.roll(p_extra, 64, 1))
    profile = jnp.concatenate([p_own, p_extra], axis=1)
    cols = iota((1, 2 * local), 1)
    work_ref[...] = kinetic_ref[...]
    for which in range(2):
        mine = (cols < local) | ((cols - local) // 64 == which)
        for i in range(4):
            row = (VALUE[i] / KIN) * profile[0:1] + (SLOPE[i] / KIN) * profile[1:2]
            at = local + 64 * which + 32 + i
            row = jnp.where(mine, row, 0.0) + work_ref[which, at : at + 1, :]
            high = row.astype(BF16).astype(F32)
            work_ref[which, at : at + 1, :] = high
            at = local + 64 * which + 32 + INNER + i
            work_ref[which, at : at + 1, :] = row - high
    matrix_ref[...] = work_ref[...].astype(BF16)
    radii = lane_radii(first, local)
    drive = field_ref[0] * radii
    for power in range(1, ORDER + 1):
        mix(coupling_ref, stack_ref, mixed_ref, (1,) if power == 1 else (0, 1, 2))
        stencil(stack_ref, matrix_ref, moved_ref)
        advance(v_ref, state_ref, stack_ref, mixed_ref, moved_ref, pot_ref, drive, time_step / power)
    split_store(stack_ref, 0, state_ref[...])
    mix(coupling_ref, stack_ref, mixed_ref, (0, 1, 2))
    part_ref[...] = jnp.zeros(part_ref.shape, F32)
    for n, value in ((0, part_in_ref[0:1, :]), (1, intersect(state_ref, mixed_ref, radii))):
        whole = jnp.sum(value, axis=1, keepdims=True) * scaling
        part_ref[n : n + 1, :] = jnp.broadcast_to(whole, (1, local))
    v_ref[...] = state_ref[...]


def later_kernel(
    first_ref,
    field_ref,
    after_ref,
    matrix_ref,
    coupling_ref,
    pot_ref,
    v_in_ref,
    stack_in_ref,
    mixed_in_ref,
    total_in_ref,
    v_ref,
    stack_ref,
    mixed_ref,
    total_ref,
    kept_ref,
    moved_ref,
    *,
    power,
):
    del v_in_ref, stack_in_ref, mixed_in_ref, total_in_ref
    kept_ref[...] = after_ref[...]
    radii = lane_radii(first_ref[0], 128)
    drive = field_ref[1] * radii
    stencil(stack_ref, matrix_ref, moved_ref)
    advance(v_ref, total_ref, stack_ref, mixed_ref, moved_ref, pot_ref, drive, time_step / power)
    mix(coupling_ref, stack_ref, mixed_ref, (0, 1, 2) if power + 1 < ORDER else (0, 2))


def last_kernel(
    first_ref,
    field_ref,
    after_ref,
    matrix_ref,
    pot_ref,
    v_ref,
    stack_ref,
    mixed_ref,
    total_ref,
    out_ref,
    moved_ref,
):
    del after_ref
    local = 128
    radii = lane_radii(first_ref[0], local)
    drive = field_ref[1] * radii
    stencil(stack_ref, matrix_ref, moved_ref)
    channels = v_ref.shape[0]
    scale = time_step / ORDER
    for c0 in range(0, channels, 80):
        rows = slice(c0, c0 + 80)
        for source, target, sign in ((1, 0, 1.0), (0, 1, -1.0), (3, 2, 1.0), (2, 3, -1.0)):
            cut = slice(OWN[PARTS[source]], OWN[PARTS[source]] + local)
            into = slice(OWN[PARTS[target]], OWN[PARTS[target]] + local)
            value = (
                KIN * moved_ref[source, rows, :local]
                + pot_ref[rows, :local] * v_ref[rows, cut]
                + drive[:, :local] * mixed_ref[rows, cut]
            )
            out_ref[target, rows, :] = total_ref[rows, into] + (sign * scale) * value


def tree(count):
    if count == 16:
        return [[2], [4, 8, 12]]
    return [[1 << k] for k in range(1, (count - 1).bit_length())]


def swaps(start, count):
    return [(start + i, 1 - 2 * (i % 2)) for i in range(count)]


def vmem(count):
    return [pl.BlockSpec(memory_space=pltpu.VMEM)] * count


def smem(count):
    return [pl.BlockSpec(memory_space=pltpu.SMEM)] * count


def params():
    return pltpu.CompilerParams(vmem_limit_bytes=32 * 1024 * 1024)


def per_device(states, dipole, pattern, angular, thresholds, surface_profile, pulse_field, *, count):
    channels, local = states.shape[1:]
    grid_points = local * count
    half = channels // 2
    axis = "radius"
    here = lax.axis_index(axis)
    first = (here * local).reshape(1).astype(jnp.int32)
    shape = jax.ShapeDtypeStruct
    width = 6 * local
    scaling = 1.0 / (math.sqrt(channels * grid_points) * (inner_radius + grid_points * spacing))

    near, far, inner = pl.pallas_call(
        pack_kernel,
        out_shape=(
            shape((half + 8, local), F32),
            shape((half + 8, local), F32),
            shape((half + 40, local), F32),
        ),
        in_specs=smem(1) + [pl.BlockSpec(memory_space=pltpu.HBM)] * 2,
        out_specs=tuple(vmem(3)),
        scratch_shapes=[
            pltpu.VMEM(states.shape, F32),
            pltpu.VMEM(surface_profile.shape, F32),
            pltpu.SemaphoreType.DMA((5,)),
        ],
        compiler_params=params(),
        name="pack",
    )(
        first,
        pltpu.with_memory_space_constraint(states, pltpu.HBM),
        pltpu.with_memory_space_constraint(surface_profile, pltpu.HBM),
    )

    coupling, kinetic, pot, v, stack, mixed, part = pl.pallas_call(
        functools.partial(table_kernel, grid_points=grid_points),
        out_shape=(
            shape((channels, 3 * channels), BF16),
            shape((2, 2 * local, 2 * local), F32),
            shape((channels, 2 * local), F32),
            shape((channels, width), F32),
            shape((3 * channels, width), BF16),
            shape((channels, width), F32),
            shape((8, local), F32),
        ),
        in_specs=smem(1) + vmem(5),
        out_specs=tuple(vmem(7)),
        compiler_params=params(),
        name="tables",
    )(first, dipole, pattern, angular.reshape(1, channels), thresholds.reshape(1, channels), states)

    far = lax.ppermute(far, axis, [(i, i + d) for i, d in swaps(1, count - 2)])
    have = [0]
    for offsets in tree(count):
        fresh, chosen = [], inner
        for offset in offsets:
            pairs = [(h, h + offset) for h in have if h + offset < count]
            got = lax.ppermute(inner, axis, pairs)
            to = [p[1] for p in pairs]
            hit = functools.reduce(jnp.logical_or, [here == t for t in to])
            chosen = jnp.where(hit, got, chosen)
            fresh += to
        if len(have) == 1:
            chosen, far = lax.optimization_barrier((chosen, far))
        inner = chosen
        have += fresh
    sent = jnp.concatenate([inner, near])
    got = lax.ppermute(sent, axis, [(i, i + d) for i, d in swaps(0, count)])

    moved = pltpu.VMEM((4, channels, 2 * local), F32)
    evolved = (
        shape((channels, width), F32),
        shape((3 * channels, width), BF16),
        shape((channels, width), F32),
        shape((channels, width), F32),
    )
    v, stack, mixed, total, matrix, part = pl.pallas_call(
        functools.partial(first_kernel, scaling=scaling),
        out_shape=evolved + (shape((2, 2 * local, 2 * local), BF16), shape((8, local), F32)),
        in_specs=smem(2) + vmem(11),
        out_specs=tuple(vmem(6)),
        scratch_shapes=[moved, pltpu.VMEM((2, 2 * local, 2 * local), F32)],
        input_output_aliases={10: 0, 11: 1, 12: 2},
        compiler_params=params(),
        name="first",
    )(first, pulse_field, far, got, sent, surface_profile, coupling, kinetic, pot, part, v, stack, mixed)

    rounds = (count - 1).bit_length()
    for power in range(1, ORDER + 1):
        low, high = rounds * (power - 1) // ORDER, rounds * power // ORDER
        before = part
        for bit in range(low, high - 1):
            before = before + lax.ppermute(before, axis, [(i, i ^ (1 << bit)) for i in range(count)])
        got = lax.ppermute(before, axis, [(i, i ^ (1 << (high - 1))) for i in range(count)])
        if power < ORDER:
            v, stack, mixed, total, kept = pl.pallas_call(
                functools.partial(later_kernel, power=power),
                out_shape=evolved + (shape(part.shape, F32),),
                in_specs=smem(2) + vmem(8),
                out_specs=tuple(vmem(5)),
                scratch_shapes=[moved],
                input_output_aliases={6: 0, 7: 1, 8: 2, 9: 3},
                compiler_params=params(),
                name="later",
            )(first, pulse_field, before, matrix, coupling, pot, v, stack, mixed, total)
            part = kept + got
        else:
            final = pl.pallas_call(
                last_kernel,
                out_shape=shape(states.shape, F32),
                in_specs=smem(2) + vmem(7),
                out_specs=vmem(1)[0],
                scratch_shapes=[moved],
                compiler_params=params(),
                name="last",
            )(first, pulse_field, before, matrix, pot, v, stack, mixed, total)
            part = before + got
    return final, part[:STEPS, 0]


def solution(mesh):
    return jax.shard_map(
        functools.partial(per_device, count=mesh.shape["radius"]),
        mesh=mesh,
        in_specs=(P("groups", None, "radius"), P(), P(), P(), P(), P(None, "radius"), P("groups")),
        out_specs=(P("groups", None, "radius"), P("groups")),
        check_vma=False,
    )
```

```python
import functools
import math

import jax
import jax.numpy as jnp
from jax import lax
from jax.experimental import pallas as pl
from jax.experimental.pallas import tpu as pltpu
from jax.sharding import PartitionSpec as P

STEPS = 2
ORDER = 4

inner_radius = 20.0
spacing = 0.08
time_step = 0.005

HALO = 2 * ORDER * STEPS
INNER = 2 * ORDER * STEPS + 2
KIN = 1.0 / (24.0 * spacing * spacing)
VALUE = (4.0, -6.0, 4.0, -1.0)
SLOPE = (-13.0 / 3.0, 9.5, -7.0, 11.0 / 6.0)

F32 = jnp.float32
BF16 = jnp.bfloat16

OWN = {"a": 0, "b": 128, "c": 512, "d": 640}
EXTRA = {"a": 256, "c": 256, "b": 384, "d": 384}
PARTS = ("a", "b", "c", "d")


def iota(shape, dim):
    return lax.broadcasted_iota(jnp.int32, shape, dim)


def is_odd(first, local):
    return lax.rem(lax.div(first, local), 2) == 1


def pack_kernel(first_ref, states_any, profile_any, near_ref, far_ref, inner_ref, states_ref, profile_ref, sems):
    channels = states_ref.shape[1]
    half = channels // 2
    local = states_ref.shape[2]
    copies = [pltpu.make_async_copy(states_any.at[k], states_ref.at[k], sems.at[k]) for k in range(4)]
    copies.append(pltpu.make_async_copy(profile_any, profile_ref, sems.at[4]))
    for copy in copies:
        copy.start()
    copies[4].wait()
    odd = is_odd(first_ref[0], local)
    zeros = jnp.zeros((6, local), F32)
    prof = profile_ref[...]
    turned = pltpu.roll(prof, HALO, 1)
    for ref, value in (
        (near_ref, jnp.where(odd, prof, turned)),
        (far_ref, jnp.where(odd, turned, prof)),
        (inner_ref, prof),
    ):
        ref[half : half + 2, :] = value
        ref[half + 2 : half + 8, :] = zeros
    group = iota((half, local), 1) // 16
    pair = (iota((channels, local), 1) & 63) // 2
    right = left = more = None
    for k, first in ((0, 0), (2, 64), (1, 16), (3, 80)):
        copies[k].wait()
        for h in range(2):
            rows = states_ref[k, half * h : half * h + half, :]
            at = first + 32 * h
            hit = group == at // 16
            shift = (at + HALO) % local
            moved = pltpu.roll(rows, shift, 1) if shift else rows
            right = moved if right is None else jnp.where(hit, moved, right)
            moved = pltpu.roll(rows, at, 1) if at else rows
            left = moved if left is None else jnp.where(hit, moved, left)
        at = 64 * (k // 2) + 2 * (k % 2)
        moved = pltpu.roll(states_ref[k], (at - 16) % local, 1)
        more = moved if more is None else jnp.where(pair == k % 2, jnp.where(iota((channels, local), 1) // 64 == k // 2, moved, more), more)
    near_ref[:half, :] = jnp.where(odd, left, right)
    far_ref[:half, :] = jnp.where(odd, right, left)
    inner_ref[:half, :] = left
    rest = None
    quad = (iota((32, local), 1) & 63) // 4
    for i in range((channels + 31) // 32):
        rows = more[32 * i : min(32 * i + 32, channels)]
        if rows.shape[0] < 32:
            rows = jnp.concatenate([rows, jnp.zeros((32 - rows.shape[0], local), F32)], axis=0)
        moved = pltpu.roll(rows, 4 * i, 1) if i else rows
        rest = moved if rest is None else jnp.where(quad == i, moved, rest)
    inner_ref[half + 8 :, :] = rest


def lane_points(lanes, first, local):
    e = (lanes - local) & 63
    own = lanes < local
    point = jnp.where(
        own,
        first + lanes,
        jnp.where(
            e < 16,
            first - 16 + e,
            jnp.where(
                e < 32,
                first + local + e - 16,
                jnp.where(e < 32 + INNER, e - 32, e - 32 - INNER),
            ),
        ),
    )
    segment = jnp.where(
        own, 0, jnp.where(e < 32, 0, jnp.where(e < 32 + INNER, 1, jnp.where(e < 36 + INNER, 2, 3)))
    )
    return point, segment


def lane_radii(first, local):
    lanes = iota((8, 2 * local), 1)
    point, _ = lane_points(lanes, first, local)
    return (inner_radius + (point + 1).astype(F32) * spacing)[:1]


def table_kernel(
    first_ref,
    dipole_ref,
    pattern_ref,
    angular_ref,
    thr_ref,
    states_ref,
    coupling_ref,
    kinetic_ref,
    pot_ref,
    stack_ref,
    mixed_ref,
    part_ref,
    *,
    grid_points,
):
    channels = dipole_ref.shape[0]
    blocks = pattern_ref.shape[0]
    size = channels // blocks
    local = 128
    first = first_ref[0]
    pattern = pattern_ref[...].astype(F32)
    joined = jnp.maximum(pattern, pattern.T).astype(BF16)
    tall = (iota((channels, blocks), 0) // size == iota((channels, blocks), 1)).astype(F32).astype(BF16)
    wide = (iota((blocks, channels), 1) // size == iota((blocks, channels), 0)).astype(F32).astype(BF16)
    rows = jnp.dot(tall, joined, preferred_element_type=F32).astype(BF16)
    mask = jnp.dot(rows, wide, preferred_element_type=F32)
    ang = jnp.broadcast_to(angular_ref[...].astype(F32), (channels, channels))
    angt = ang.T
    allowed = (mask > 0.5) & (jnp.abs(ang - angt) == 1.0)
    dip = dipole_ref[...]
    coupling = jnp.where(allowed, 0.5 * (dip + dip.T), 0.0)
    high = coupling.astype(BF16)
    low = (coupling - high.astype(F32)).astype(BF16)
    coupling_ref[...] = jnp.concatenate([high, high, low], axis=1)
    radii = lane_radii(first, local)
    inverse = 1.0 / (radii * radii)
    centrifugal = 0.5 * angt[:, :local] * (angt[:, :local] + 1.0)
    thr = jnp.broadcast_to(thr_ref[...], (local, channels)).T
    pot_ref[:, :local] = thr + centrifugal * inverse[:, :local]
    pot_ref[:, local:] = thr + centrifugal * inverse[:, local:]
    shape = (2 * local, 2 * local)
    src, dst = iota(shape, 0), iota(shape, 1)
    sp, ss = lane_points(src, first, local)
    dp, ds = lane_points(dst, first, local)
    gap = jnp.abs(sp - dp)
    coef = jnp.where(gap == 0, 30.0, jnp.where(gap == 1, -16.0, jnp.where(gap == 2, 1.0, 0.0)))
    same = (ss < 2) & (ss == jnp.minimum(ds, 1))
    valid = (dp >= 0) & (dp < grid_points) & (ds < 3)
    coef = jnp.where(same & valid, coef, 0.0)
    for which in range(2):
        mine = (src < local) | ((src - local) // 64 == which)
        mine = mine & ((dst < local) | ((dst - local) // 64 == which))
        kinetic_ref[which] = jnp.where(mine, coef, 0.0)
    for k, part in enumerate(PARTS):
        split_store(stack_ref, OWN[part], states_ref[k])
    mix(coupling_ref, stack_ref, mixed_ref, (0, 2))
    part_ref[0:1, :] = intersect(states_ref[2], states_ref[3], mixed_ref, radii)
    part_ref[1:, :] = jnp.zeros((part_ref.shape[0] - 1, local), F32)


def split_store(stack_ref, at, value):
    channels = value.shape[0]
    width = value.shape[1]
    high = value.astype(BF16)
    low = (value - high.astype(F32)).astype(BF16)
    stack_ref[:channels, at : at + width] = high
    stack_ref[channels : 2 * channels, at : at + width] = low
    stack_ref[2 * channels :, at : at + width] = high


def mix(coupling_ref, stack_ref, mixed_ref, tiles):
    for n in tiles:
        cut = slice(256 * n, 256 * n + 256)
        mixed_ref[:, cut] = jnp.dot(coupling_ref[...], stack_ref[:, cut], preferred_element_type=F32)


def stencil(stack_ref, matrix_ref, moved_ref, parts):
    channels = stack_ref.shape[0] // 3
    for part in parts:
        own, extra = OWN[part], EXTRA[part]
        weights = matrix_ref[0 if part in "ab" else 1]
        total = None
        for rows in (slice(0, channels), slice(channels, 2 * channels)):
            left = jnp.concatenate([stack_ref[rows, own : own + 128], stack_ref[rows, extra : extra + 128]], axis=1)
            got = jnp.dot(left, weights, preferred_element_type=F32)
            total = got if total is None else total + got
        moved_ref[PARTS.index(part)] = total


def advance(targets, old, keep, mixed_ref, moved_ref, pot_ref, drive, scale, chunk=80):
    channels, local = pot_ref.shape[0], 128
    own, extra = slice(0, local), slice(local, 2 * local)
    for c0 in range(0, channels, chunk):
        rows = slice(c0, c0 + chunk)
        for target in targets:
            sign = 1.0 if target in ("a", "c", "ac") else -1.0
            if len(target) == 1:
                source = {"a": "b", "b": "a", "c": "d", "d": "c"}[target]
                to, at, lanes = OWN[target], OWN[source], own
                moved = moved_ref[PARTS.index(source), rows, own]
            else:
                k, m = (1, 3) if target == "ac" else (0, 2)
                to, at, lanes = EXTRA[target[0]], EXTRA[PARTS[k]], extra
                moved = moved_ref[k, rows, extra] + moved_ref[m, rows, extra]
            factor = sign * scale
            value = (
                (factor * KIN) * moved
                + (factor * pot_ref[rows, lanes]) * old(at, rows)
                + (factor * drive[:, lanes]) * mixed_ref[rows, at : at + local]
            )
            keep(to, rows, value)


def split_rows(stack_ref, at, rows, value):
    channels = stack_ref.shape[0] // 3
    high = value.astype(BF16)
    low = (value - high.astype(F32)).astype(BF16)
    cut = slice(at, at + value.shape[1])
    stack_ref[rows, cut] = high
    stack_ref[channels + rows.start : channels + rows.stop, cut] = low
    stack_ref[2 * channels + rows.start : 2 * channels + rows.stop, cut] = high


def intersect(third, fourth, mixed_ref, radii):
    def mixed(part):
        return mixed_ref[:, OWN[part] : OWN[part] + 128]

    both = third * mixed("b") - fourth * mixed("a")
    return jnp.sum(both * radii[:, :128], axis=0, keepdims=True)


def first_kernel(
    first_ref,
    field_ref,
    far_ref,
    got_ref,
    sent_ref,
    profile_ref,
    states_ref,
    coupling_ref,
    kinetic_ref,
    pot_ref,
    part_in_ref,
    stack_in_ref,
    mixed_in_ref,
    stack_ref,
    mixed_ref,
    state_ref,
    matrix_ref,
    part_ref,
    v_ref,
    other_v_ref,
    other_stack_ref,
    moved_ref,
    work_ref,
    *,
    scaling,
):
    del stack_in_ref, mixed_in_ref
    channels = v_ref.shape[0]
    half = channels // 2
    local = 128
    first = first_ref[0]
    odd = is_odd(first, local)
    split = half + 40
    inner = jnp.where(odd, got_ref[:split, :], sent_ref[:split, :])
    left = jnp.where(odd, got_ref[split:, :], far_ref[...])
    right = jnp.where(odd, far_ref[...], got_ref[split:, :])
    lanes = iota((half, local), 1) & 63
    for pair, at in ((0, 256), (1, 384)):
        for h in range(2):
            back = 16 * pair + 32 * h

            def rolled(value, to):
                shift = (to - back) % local
                return pltpu.roll(value, shift, 1) if shift else value

            value = jnp.where(
                lanes < 16,
                rolled(left[:half, :], 0),
                jnp.where(
                    lanes < 32,
                    rolled(right[:half, :], 16),
                    jnp.where(
                        lanes < 48,
                        rolled(inner[:half, :], 32),
                        jnp.where(
                            (lanes >= 50) & (lanes < 54), rolled(inner[:half, :], 50), jnp.zeros((half, local), F32)
                        ),
                    ),
                ),
            )
            v_ref[half * h : half * h + half, at : at + local] = value
        narrow = iota((32, local), 1) & 63
        for i in range((channels + 31) // 32):
            rows = slice(32 * i, min(32 * i + 32, channels))
            count = rows.stop - rows.start
            value = pltpu.roll(inner[half + 8 : half + 8 + count, :], (48 - 4 * i - 2 * pair) % local, 1)
            hit = (narrow[:count] >= 48) & (narrow[:count] < 50)
            v_ref[rows, at : at + local] = jnp.where(hit, value, v_ref[rows, at : at + local])
    split_store(stack_ref, 256, v_ref[:, 256:512])
    p_own = profile_ref[...]
    lanes2 = iota((2, local), 1)
    inner_profile = inner[half : half + 2, :]
    p_extra = jnp.where(
        lanes2 < 16,
        left[half : half + 2, :],
        jnp.where(
            lanes2 < 32,
            pltpu.roll(right[half : half + 2, :], 16, 1),
            jnp.where(
                lanes2 < 32 + INNER,
                pltpu.roll(inner_profile, 32, 1),
                jnp.where(lanes2 < 36 + INNER, pltpu.roll(inner_profile, 32 + INNER, 1), 0.0),
            ),
        ),
    )
    p_extra = jnp.where(lanes2 < 64, p_extra, pltpu.roll(p_extra, 64, 1))
    profile = jnp.concatenate([p_own, p_extra], axis=1)
    cols = iota((1, 2 * local), 1)
    work_ref[...] = kinetic_ref[...]
    for which in range(2):
        mine = (cols < local) | ((cols - local) // 64 == which)
        for i in range(4):
            row = (VALUE[i] / KIN) * profile[0:1] + (SLOPE[i] / KIN) * profile[1:2]
            at = local + 64 * which + 32 + i
            row = jnp.where(mine, row, 0.0) + work_ref[which, at : at + 1, :]
            high = row.astype(BF16).astype(F32)
            work_ref[which, at : at + 1, :] = high
            at = local + 64 * which + 32 + INNER + i
            work_ref[which, at : at + 1, :] = row - high
    matrix_ref[...] = work_ref[...].astype(BF16)
    radii = lane_radii(first, local)
    drive = field_ref[0] * radii
    own_at = {OWN[part]: k for k, part in enumerate(PARTS)}
    vs, stacks = (v_ref, other_v_ref), (stack_ref, other_stack_ref)
    for power in range(1, ORDER + 1):
        v, stack = vs[1 - power % 2], stacks[1 - power % 2]
        next_v, next_stack = vs[power % 2], stacks[power % 2]

        def old(at, rows):
            if power == 1 and at in own_at:
                return states_ref[own_at[at], rows, :]
            return v[rows, at : at + local]

        def keep(at, rows, value):
            cut = slice(at, at + local)
            before = old(at, rows) if power == 1 else state_ref[rows, cut]
            state_ref[rows, cut] = before + value
            if power < ORDER:
                next_v[rows, cut] = value
                split_rows(next_stack, at, rows, value)
            else:
                split_rows(next_stack, at, rows, before + value)

        scale = time_step / power
        mix(coupling_ref, stack, mixed_ref, (1,) if power == 1 else (0, 2, 1))
        stencil(stack, matrix_ref, moved_ref, "ab")
        advance("ab", old, keep, mixed_ref, moved_ref, pot_ref, drive, scale)
        stencil(stack, matrix_ref, moved_ref, "cd")
        advance("cd", old, keep, mixed_ref, moved_ref, pot_ref, drive, scale)
        advance(("ac", "bd"), old, keep, mixed_ref, moved_ref, pot_ref, drive, scale)
    mix(coupling_ref, stack_ref, mixed_ref, (0,))
    part_ref[...] = jnp.zeros(part_ref.shape, F32)
    state = [state_ref[:, OWN[part] : OWN[part] + local] for part in "cd"]
    for n, value in ((0, part_in_ref[0:1, :]), (1, intersect(state[0], state[1], mixed_ref, radii))):
        whole = jnp.sum(value, axis=1, keepdims=True) * scaling
        part_ref[n : n + 1, :] = jnp.broadcast_to(whole, (1, local))


def later_kernel(
    first_ref,
    field_ref,
    after_ref,
    matrix_ref,
    coupling_ref,
    pot_ref,
    v_in_ref,
    stack_in_ref,
    mixed_in_ref,
    total_in_ref,
    v_ref,
    stack_ref,
    mixed_ref,
    total_ref,
    kept_ref,
    moved_ref,
    now_ref,
    *,
    power,
):
    kept_ref[...] = after_ref[...]
    local = 128
    radii = lane_radii(first_ref[0], local)
    drive = field_ref[1] * radii

    def old(at, rows):
        return v_in_ref[rows, at : at + local]

    def keep(at, rows, value):
        cut = slice(at, at + local)
        v_ref[rows, cut] = value
        split_rows(stack_ref, at, rows, value)
        if at in OWN.values():
            total_ref[rows, cut] = total_in_ref[rows, cut] + value

    scale = time_step / power
    mix(coupling_ref, stack_in_ref, now_ref, (2, 1))
    stencil(stack_in_ref, matrix_ref, moved_ref, "ab")
    advance("ab", old, keep, mixed_in_ref, moved_ref, pot_ref, drive, scale)
    stencil(stack_in_ref, matrix_ref, moved_ref, "cd")
    advance("cd", old, keep, now_ref, moved_ref, pot_ref, drive, scale)
    advance(("ac", "bd"), old, keep, now_ref, moved_ref, pot_ref, drive, scale)
    mix(coupling_ref, stack_ref, mixed_ref, (0, 2, 1))


def rest_kernel(
    first_ref,
    field_ref,
    after_ref,
    matrix_ref,
    coupling_ref,
    pot_ref,
    v_in_ref,
    stack_in_ref,
    mixed_in_ref,
    total_in_ref,
    out_any,
    v_ref,
    other_v_ref,
    stack_ref,
    other_stack_ref,
    mixed_ref,
    total_ref,
    moved_ref,
    sems,
):
    del after_ref
    local = 128
    radii = lane_radii(first_ref[0], local)
    drive = field_ref[1] * radii
    own_at = {OWN[part]: k for k, part in enumerate(PARTS)}
    vs, stacks = (v_ref, other_v_ref), (stack_ref, other_stack_ref)
    copies = [pltpu.make_async_copy(total_ref.at[k], out_any.at[k], sems.at[k]) for k in range(4)]
    for power in range(2, ORDER + 1):
        v, stack = vs[power % 2], stacks[power % 2]
        next_v, next_stack = vs[1 - power % 2], stacks[1 - power % 2]
        if power == 2:
            v, stack = v_in_ref, stack_in_ref
        mixed = mixed_in_ref if power == 2 else mixed_ref
        final = power == ORDER

        def old(at, rows):
            return v[rows, at : at + local]

        def keep(at, rows, value):
            cut = slice(at, at + local)
            if not final:
                next_v[rows, cut] = value
                split_rows(next_stack, at, rows, value)
            if at in own_at:
                k = own_at[at]
                before = total_in_ref[rows, cut] if power == 2 else total_ref[k, rows, :]
                total_ref[k, rows, :] = before + value

        scale = time_step / power
        if power > 2:
            mix(coupling_ref, stack, mixed_ref, (0, 2) if final else (0, 2, 1))
        for pair in ("ab", "cd"):
            stencil(stack, matrix_ref, moved_ref, pair)
            advance(pair, old, keep, mixed, moved_ref, pot_ref, drive, scale)
            if final:
                for part in pair:
                    copies[PARTS.index(part)].start()
        if not final:
            advance(("ac", "bd"), old, keep, mixed, moved_ref, pot_ref, drive, scale)
    for copy in copies:
        copy.wait()


def tree(count):
    if count == 16:
        return [[2], [4, 8, 12]]
    return [[1 << k] for k in range(1, (count - 1).bit_length())]


def swaps(start, count):
    return [(start + i, 1 - 2 * (i % 2)) for i in range(count)]


def full_cycle(pairs, count):
    to = {i: i ^ 1 for i in range(count)}
    for a, b in pairs:
        to[a], to[b], to[b ^ 1], to[a ^ 1] = b, b ^ 1, a ^ 1, a
    return sorted(to.items())


def vmem(count):
    return [pl.BlockSpec(memory_space=pltpu.VMEM)] * count


def smem(count):
    return [pl.BlockSpec(memory_space=pltpu.SMEM)] * count


def params():
    return pltpu.CompilerParams(vmem_limit_bytes=32 * 1024 * 1024)


def per_device(states, dipole, pattern, angular, thresholds, surface_profile, pulse_field, *, count):
    channels, local = states.shape[1:]
    grid_points = local * count
    half = channels // 2
    axis = "radius"
    here = lax.axis_index(axis)
    first = (here * local).reshape(1).astype(jnp.int32)
    shape = jax.ShapeDtypeStruct
    width = 6 * local
    scaling = 1.0 / (math.sqrt(channels * grid_points) * (inner_radius + grid_points * spacing))

    near, far, inner = pl.pallas_call(
        pack_kernel,
        out_shape=(
            shape((half + 8, local), F32),
            shape((half + 8, local), F32),
            shape((half + 40, local), F32),
        ),
        in_specs=smem(1) + [pl.BlockSpec(memory_space=pltpu.HBM)] * 2,
        out_specs=tuple(vmem(3)),
        scratch_shapes=[
            pltpu.VMEM(states.shape, F32),
            pltpu.VMEM(surface_profile.shape, F32),
            pltpu.SemaphoreType.DMA((5,)),
        ],
        compiler_params=params(),
        name="pack",
    )(
        first,
        pltpu.with_memory_space_constraint(states, pltpu.HBM),
        pltpu.with_memory_space_constraint(surface_profile, pltpu.HBM),
    )

    coupling, kinetic, pot, stack, mixed, part = pl.pallas_call(
        functools.partial(table_kernel, grid_points=grid_points),
        out_shape=(
            shape((channels, 3 * channels), BF16),
            shape((2, 2 * local, 2 * local), F32),
            shape((channels, 2 * local), F32),
            shape((3 * channels, width), BF16),
            shape((channels, width), F32),
            shape((8, local), F32),
        ),
        in_specs=smem(1) + vmem(5),
        out_specs=tuple(vmem(6)),
        compiler_params=params(),
        name="tables",
    )(first, dipole, pattern, angular.reshape(1, channels), thresholds.reshape(1, channels), states)

    far = lax.ppermute(far, axis, [(i, i + d) for i, d in swaps(1, count - 2)])
    have, far_waits = [0], True
    for offsets in tree(count):
        fresh, chosen = [], inner
        for offset in offsets:
            pairs = [(h, h + offset) for h in have if h + offset < count]
            got = lax.ppermute(inner, axis, full_cycle(pairs, count))
            to = [p[1] for p in pairs]
            hit = functools.reduce(jnp.logical_or, [here == t for t in to])
            chosen = jnp.where(hit, got, chosen)
            fresh += to
        if len(have) > 1 and far_waits:
            chosen, far = lax.optimization_barrier((chosen, far))
            far_waits = False
        inner = chosen
        have += fresh
    sent = jnp.concatenate([inner, near])
    got = lax.ppermute(sent, axis, [(i, i + d) for i, d in swaps(0, count)])

    moved = pltpu.VMEM((4, channels, 2 * local), F32)
    evolved = (
        shape((channels, width), F32),
        shape((3 * channels, width), BF16),
        shape((channels, width), F32),
        shape((channels, width), F32),
    )
    stack, mixed, total, matrix, part = pl.pallas_call(
        functools.partial(first_kernel, scaling=scaling),
        out_shape=evolved[1:] + (shape((2, 2 * local, 2 * local), BF16), shape((8, local), F32)),
        in_specs=smem(2) + vmem(11),
        out_specs=tuple(vmem(5)),
        scratch_shapes=[
            pltpu.VMEM((channels, width), F32),
            pltpu.VMEM((channels, width), F32),
            pltpu.VMEM((3 * channels, width), BF16),
            moved,
            pltpu.VMEM((2, 2 * local, 2 * local), F32),
        ],
        input_output_aliases={11: 0, 12: 1},
        compiler_params=params(),
        name="first",
    )(first, pulse_field, far, got, sent, surface_profile, states, coupling, kinetic, pot, part, stack, mixed)

    bits = (count - 1).bit_length()
    groups = [range(low, min(low + 2, bits)) for low in range(0, bits, 2)]

    def send(value, group):
        low = group[0]
        return [
            lax.ppermute(value, axis, [(i, i ^ (pattern << low)) for i in range(count)])
            for pattern in range(1, 1 << len(group))
        ]

    def add(value, got):
        if len(got) == 1:
            return value + got[0]
        return (value + got[0]) + (got[1] + got[2])

    got = send(part, groups[0])
    v, stack, mixed, total, part = pl.pallas_call(
        functools.partial(later_kernel, power=1),
        out_shape=evolved + (shape(part.shape, F32),),
        in_specs=smem(2) + vmem(8),
        out_specs=tuple(vmem(5)),
        scratch_shapes=[moved, pltpu.VMEM((channels, width), F32)],
        compiler_params=params(),
        name="later",
    )(first, pulse_field, part, matrix, coupling, pot, total, stack, mixed, total)
    part = add(part, got)
    for group in groups[1:-1]:
        part = add(part, send(part, group))
    got = send(part, groups[-1])
    final = pl.pallas_call(
        rest_kernel,
        out_shape=shape(states.shape, F32),
        in_specs=smem(2) + vmem(8),
        out_specs=pl.BlockSpec(memory_space=pltpu.HBM),
        scratch_shapes=[
            pltpu.VMEM((channels, width), F32),
            pltpu.VMEM((channels, width), F32),
            pltpu.VMEM((3 * channels, width), BF16),
            pltpu.VMEM((3 * channels, width), BF16),
            pltpu.VMEM((channels, width), F32),
            pltpu.VMEM(states.shape, F32),
            moved,
            pltpu.SemaphoreType.DMA((4,)),
        ],
        compiler_params=params(),
        name="rest",
    )(first, pulse_field, part, matrix, coupling, pot, v, stack, mixed, total)
    part = add(part, got)
    return final, part[:STEPS, 0]


def solution(mesh):
    return jax.shard_map(
        functools.partial(per_device, count=mesh.shape["radius"]),
        mesh=mesh,
        in_specs=(P("groups", None, "radius"), P(), P(), P(), P(), P(None, "radius"), P("groups")),
        out_specs=(P("groups", None, "radius"), P("groups")),
        check_vma=False,
    )
```

```python
import functools
import math

import jax
import jax.numpy as jnp
from jax import lax
from jax.experimental import pallas as pl
from jax.experimental.pallas import tpu as pltpu
from jax.sharding import PartitionSpec as P

STEPS = 2
ORDER = 4

inner_radius = 20.0
spacing = 0.08
time_step = 0.005

HALO = 2 * ORDER * STEPS
INNER = 2 * ORDER * STEPS + 2
KIN = 1.0 / (24.0 * spacing * spacing)
VALUE = (4.0, -6.0, 4.0, -1.0)
SLOPE = (-13.0 / 3.0, 9.5, -7.0, 11.0 / 6.0)

F32 = jnp.float32
BF16 = jnp.bfloat16

OWN = {"a": 0, "b": 128, "c": 512, "d": 640}
EXTRA = {"a": 256, "c": 256, "b": 384, "d": 384}
PARTS = ("a", "b", "c", "d")


def iota(shape, dim):
    return lax.broadcasted_iota(jnp.int32, shape, dim)


def is_odd(first, local):
    return lax.rem(lax.div(first, local), 2) == 1


def pack_kernel(first_ref, states_any, profile_any, near_ref, far_ref, inner_ref, states_ref, profile_ref, sems):
    channels = states_ref.shape[1]
    half = channels // 2
    local = states_ref.shape[2]
    copies = [pltpu.make_async_copy(states_any.at[k], states_ref.at[k], sems.at[k]) for k in range(4)]
    copies.append(pltpu.make_async_copy(profile_any, profile_ref, sems.at[4]))
    for copy in copies:
        copy.start()
    copies[4].wait()
    odd = is_odd(first_ref[0], local)
    zeros = jnp.zeros((6, local), F32)
    prof = profile_ref[...]
    turned = pltpu.roll(prof, HALO, 1)
    for ref, value in (
        (near_ref, jnp.where(odd, prof, turned)),
        (far_ref, jnp.where(odd, turned, prof)),
        (inner_ref, prof),
    ):
        ref[half : half + 2, :] = value
        ref[half + 2 : half + 8, :] = zeros
    group = iota((half, local), 1) // HALO
    groups = local // HALO
    right = left = None
    rest = [None, None]
    for k, first in ((0, 0), (2, 64), (1, 16), (3, 80)):
        copies[k].wait()
        for h in range(2):
            at = first + 32 * h
            moved = pltpu.roll(states_ref[k, half * h : half * h + half, :], (at + HALO) % local, 1)

            def put(old, to):
                return moved if old is None else jnp.where(group == to // HALO % groups, moved, old)

            right = put(right, at)
            left = put(left, at + HALO)
            rest[h] = put(rest[h], at + 2 * HALO)
    near_ref[:half, :] = jnp.where(odd, left, right)
    far_ref[:half, :] = jnp.where(odd, right, left)
    inner_ref[:half, :] = left
    lanes = iota((32, local), 1)
    more = None
    for h in range(2):
        for i in range((half + 31) // 32):
            rows = rest[h][32 * i : min(32 * i + 32, half)]
            if rows.shape[0] < 32:
                rows = jnp.concatenate([rows, jnp.zeros((32 - rows.shape[0], local), F32)], axis=0)
            moved = pltpu.roll(rows, 2 * i, 1) if i else rows
            hit = ((lanes & 15) // 2 == i) & ((lanes & 32) == 32 * (1 - h))
            more = moved if more is None else jnp.where(hit, moved, more)
    inner_ref[half + 8 :, :] = more


def lane_points(lanes, first, local):
    e = (lanes - local) & 63
    own = lanes < local
    point = jnp.where(
        own,
        first + lanes,
        jnp.where(
            e < 16,
            first - 16 + e,
            jnp.where(
                e < 32,
                first + local + e - 16,
                jnp.where(e < 32 + INNER, e - 32, e - 32 - INNER),
            ),
        ),
    )
    segment = jnp.where(
        own, 0, jnp.where(e < 32, 0, jnp.where(e < 32 + INNER, 1, jnp.where(e < 36 + INNER, 2, 3)))
    )
    return point, segment


def lane_radii(first, local):
    lanes = iota((8, 2 * local), 1)
    point, _ = lane_points(lanes, first, local)
    return (inner_radius + (point + 1).astype(F32) * spacing)[:1]


def table_kernel(
    first_ref,
    dipole_ref,
    pattern_ref,
    angular_ref,
    thr_ref,
    states_ref,
    coupling_ref,
    kinetic_ref,
    pot_ref,
    stack_ref,
    mixed_ref,
    part_ref,
    *,
    grid_points,
):
    channels = dipole_ref.shape[0]
    blocks = pattern_ref.shape[0]
    size = channels // blocks
    local = 128
    first = first_ref[0]
    pattern = pattern_ref[...].astype(F32)
    joined = jnp.maximum(pattern, pattern.T).astype(BF16)
    tall = (iota((channels, blocks), 0) // size == iota((channels, blocks), 1)).astype(F32).astype(BF16)
    wide = (iota((blocks, channels), 1) // size == iota((blocks, channels), 0)).astype(F32).astype(BF16)
    rows = jnp.dot(tall, joined, preferred_element_type=F32).astype(BF16)
    mask = jnp.dot(rows, wide, preferred_element_type=F32)
    ang = jnp.broadcast_to(angular_ref[...].astype(F32), (channels, channels))
    angt = ang.T
    allowed = (mask > 0.5) & (jnp.abs(ang - angt) == 1.0)
    dip = dipole_ref[...]
    coupling = jnp.where(allowed, 0.5 * (dip + dip.T), 0.0)
    high = coupling.astype(BF16)
    low = (coupling - high.astype(F32)).astype(BF16)
    coupling_ref[...] = jnp.concatenate([high, high, low], axis=1)
    radii = lane_radii(first, local)
    inverse = 1.0 / (radii * radii)
    centrifugal = 0.5 * angt[:, :local] * (angt[:, :local] + 1.0)
    thr = jnp.broadcast_to(thr_ref[...], (local, channels)).T
    pot_ref[:, :local] = thr + centrifugal * inverse[:, :local]
    pot_ref[:, local:] = thr + centrifugal * inverse[:, local:]
    shape = (2 * local, 2 * local)
    src, dst = iota(shape, 0), iota(shape, 1)
    sp, ss = lane_points(src, first, local)
    dp, ds = lane_points(dst, first, local)
    gap = jnp.abs(sp - dp)
    coef = jnp.where(gap == 0, 30.0, jnp.where(gap == 1, -16.0, jnp.where(gap == 2, 1.0, 0.0)))
    same = (ss < 2) & (ss == jnp.minimum(ds, 1))
    valid = (dp >= 0) & (dp < grid_points) & (ds < 3)
    coef = jnp.where(same & valid, coef, 0.0)
    for which in range(2):
        mine = (src < local) | ((src - local) // 64 == which)
        mine = mine & ((dst < local) | ((dst - local) // 64 == which))
        kinetic_ref[which] = jnp.where(mine, coef, 0.0)
    for k, part in enumerate(PARTS):
        split_store(stack_ref, OWN[part], states_ref[k])
    mix(coupling_ref, stack_ref, mixed_ref, (0, 2))
    part_ref[0:1, :] = intersect(states_ref[2], states_ref[3], mixed_ref, radii)
    part_ref[1:, :] = jnp.zeros((part_ref.shape[0] - 1, local), F32)


def split_store(stack_ref, at, value):
    channels = value.shape[0]
    width = value.shape[1]
    high = value.astype(BF16)
    low = (value - high.astype(F32)).astype(BF16)
    stack_ref[:channels, at : at + width] = high
    stack_ref[channels : 2 * channels, at : at + width] = low
    stack_ref[2 * channels :, at : at + width] = high


def mix(coupling_ref, stack_ref, mixed_ref, tiles):
    for n in tiles:
        cut = slice(256 * n, 256 * n + 256)
        mixed_ref[:, cut] = jnp.dot(coupling_ref[...], stack_ref[:, cut], preferred_element_type=F32)


def stencil(stack_ref, matrix_ref, moved_ref, parts):
    channels = stack_ref.shape[0] // 3
    for part in parts:
        own, extra = OWN[part], EXTRA[part]
        weights = matrix_ref[0 if part in "ab" else 1]
        total = None
        for rows in (slice(0, channels), slice(channels, 2 * channels)):
            left = jnp.concatenate([stack_ref[rows, own : own + 128], stack_ref[rows, extra : extra + 128]], axis=1)
            got = jnp.dot(left, weights, preferred_element_type=F32)
            total = got if total is None else total + got
        moved_ref[PARTS.index(part)] = total


def advance(targets, old, keep, mixed_ref, moved_ref, pot_ref, drive, scale, chunk=80):
    channels, local = pot_ref.shape[0], 128
    own, extra = slice(0, local), slice(local, 2 * local)
    for c0 in range(0, channels, chunk):
        rows = slice(c0, c0 + chunk)
        for target in targets:
            sign = 1.0 if target in ("a", "c", "ac") else -1.0
            if len(target) == 1:
                source = {"a": "b", "b": "a", "c": "d", "d": "c"}[target]
                to, at, lanes = OWN[target], OWN[source], own
                moved = moved_ref[PARTS.index(source), rows, own]
            else:
                k, m = (1, 3) if target == "ac" else (0, 2)
                to, at, lanes = EXTRA[target[0]], EXTRA[PARTS[k]], extra
                moved = moved_ref[k, rows, extra] + moved_ref[m, rows, extra]
            factor = sign * scale
            value = (
                (factor * KIN) * moved
                + (factor * pot_ref[rows, lanes]) * old(at, rows)
                + (factor * drive[:, lanes]) * mixed_ref[rows, at : at + local]
            )
            keep(to, rows, value)


def split_rows(stack_ref, at, rows, value):
    channels = stack_ref.shape[0] // 3
    high = value.astype(BF16)
    low = (value - high.astype(F32)).astype(BF16)
    cut = slice(at, at + value.shape[1])
    stack_ref[rows, cut] = high
    stack_ref[channels + rows.start : channels + rows.stop, cut] = low
    stack_ref[2 * channels + rows.start : 2 * channels + rows.stop, cut] = high


def intersect(third, fourth, mixed_ref, radii):
    def mixed(part):
        return mixed_ref[:, OWN[part] : OWN[part] + 128]

    both = third * mixed("b") - fourth * mixed("a")
    return jnp.sum(both * radii[:, :128], axis=0, keepdims=True)


def first_kernel(
    first_ref,
    field_ref,
    far_ref,
    got_ref,
    sent_ref,
    profile_ref,
    states_ref,
    coupling_ref,
    kinetic_ref,
    pot_ref,
    part_in_ref,
    stack_in_ref,
    mixed_in_ref,
    stack_ref,
    mixed_ref,
    state_ref,
    matrix_ref,
    part_ref,
    v_ref,
    other_v_ref,
    other_stack_ref,
    moved_ref,
    work_ref,
    *,
    scaling,
):
    del stack_in_ref, mixed_in_ref
    channels = v_ref.shape[0]
    half = channels // 2
    local = 128
    first = first_ref[0]
    odd = is_odd(first, local)
    split = half + 40
    inner = jnp.where(odd, got_ref[:split, :], sent_ref[:split, :])
    left = jnp.where(odd, got_ref[split:, :], far_ref[...])
    right = jnp.where(odd, far_ref[...], got_ref[split:, :])
    lanes = iota((half, local), 1) & 63
    for pair, at in ((0, 256), (1, 384)):
        for h in range(2):
            back = 16 * pair + 32 * h

            def rolled(value, to):
                shift = (to - back) % local
                return pltpu.roll(value, shift, 1) if shift else value

            halo = jnp.where(((lanes - back) & 63) < 16, left[:half, :], right[:half, :])
            value = jnp.where(
                lanes < 32,
                rolled(halo, 0),
                jnp.where(
                    lanes < 48,
                    rolled(inner[:half, :], 16),
                    jnp.where((lanes >= 50) & (lanes < 54), rolled(inner[:half, :], 34), 0.0),
                ),
            )
            v_ref[half * h : half * h + half, at : at + local] = value
            narrow = iota((32, local), 1) & 63
            for i in range((half + 31) // 32):
                rows = slice(half * h + 32 * i, half * h + min(32 * i + 32, half))
                count = rows.stop - rows.start
                value = rolled(inner[half + 8 : half + 8 + count, :], 16 - 2 * i)
                hit = (narrow[:count] >= 48) & (narrow[:count] < 50)
                v_ref[rows, at : at + local] = jnp.where(hit, value, v_ref[rows, at : at + local])
    split_store(stack_ref, 256, v_ref[:, 256:512])
    p_own = profile_ref[...]
    lanes2 = iota((2, local), 1)
    inner_profile = inner[half : half + 2, :]
    p_extra = jnp.where(
        lanes2 < 16,
        left[half : half + 2, :],
        jnp.where(
            lanes2 < 32,
            pltpu.roll(right[half : half + 2, :], 16, 1),
            jnp.where(
                lanes2 < 32 + INNER,
                pltpu.roll(inner_profile, 32, 1),
                jnp.where(lanes2 < 36 + INNER, pltpu.roll(inner_profile, 32 + INNER, 1), 0.0),
            ),
        ),
    )
    p_extra = jnp.where(lanes2 < 64, p_extra, pltpu.roll(p_extra, 64, 1))
    profile = jnp.concatenate([p_own, p_extra], axis=1)
    cols = iota((1, 2 * local), 1)
    work_ref[...] = kinetic_ref[...]
    for which in range(2):
        mine = (cols < local) | ((cols - local) // 64 == which)
        for i in range(4):
            row = (VALUE[i] / KIN) * profile[0:1] + (SLOPE[i] / KIN) * profile[1:2]
            at = local + 64 * which + 32 + i
            row = jnp.where(mine, row, 0.0) + work_ref[which, at : at + 1, :]
            high = row.astype(BF16).astype(F32)
            work_ref[which, at : at + 1, :] = high
            at = local + 64 * which + 32 + INNER + i
            work_ref[which, at : at + 1, :] = row - high
    matrix_ref[...] = work_ref[...].astype(BF16)
    radii = lane_radii(first, local)
    drive = field_ref[0] * radii
    own_at = {OWN[part]: k for k, part in enumerate(PARTS)}
    vs, stacks = (v_ref, other_v_ref), (stack_ref, other_stack_ref)
    for power in range(1, ORDER + 1):
        v, stack = vs[1 - power % 2], stacks[1 - power % 2]
        next_v, next_stack = vs[power % 2], stacks[power % 2]

        def old(at, rows):
            if power == 1 and at in own_at:
                return states_ref[own_at[at], rows, :]
            return v[rows, at : at + local]

        def keep(at, rows, value):
            cut = slice(at, at + local)
            before = old(at, rows) if power == 1 else state_ref[rows, cut]
            state_ref[rows, cut] = before + value
            if power < ORDER:
                next_v[rows, cut] = value
                split_rows(next_stack, at, rows, value)
            else:
                split_rows(next_stack, at, rows, before + value)

        scale = time_step / power
        for pair, tile in (("ab", 0), ("cd", 2)):
            if power > 1:
                mix(coupling_ref, stack, mixed_ref, (tile,))
            stencil(stack, matrix_ref, moved_ref, pair)
            advance(pair, old, keep, mixed_ref, moved_ref, pot_ref, drive, scale)
        mix(coupling_ref, stack, mixed_ref, (1,))
        advance(("ac", "bd"), old, keep, mixed_ref, moved_ref, pot_ref, drive, scale)
    mix(coupling_ref, stack_ref, mixed_ref, (0,))
    part_ref[...] = jnp.zeros(part_ref.shape, F32)
    state = [state_ref[:, OWN[part] : OWN[part] + local] for part in "cd"]
    for n, value in ((0, part_in_ref[0:1, :]), (1, intersect(state[0], state[1], mixed_ref, radii))):
        whole = jnp.sum(value, axis=1, keepdims=True) * scaling
        here = (iota(part_ref.shape, 0) == 0) & (iota(part_ref.shape, 1) == n)
        part_ref[...] = jnp.where(here, whole, part_ref[...])


def later_kernel(
    first_ref,
    field_ref,
    after_ref,
    matrix_ref,
    coupling_ref,
    pot_ref,
    v_in_ref,
    stack_in_ref,
    mixed_in_ref,
    total_in_ref,
    v_ref,
    stack_ref,
    mixed_ref,
    total_ref,
    kept_ref,
    moved_ref,
    now_ref,
    *,
    power,
):
    kept_ref[...] = after_ref[...]
    local = 128
    radii = lane_radii(first_ref[0], local)
    drive = field_ref[1] * radii

    def old(at, rows):
        return v_in_ref[rows, at : at + local]

    def keep(at, rows, value):
        cut = slice(at, at + local)
        v_ref[rows, cut] = value
        split_rows(stack_ref, at, rows, value)
        if at in OWN.values():
            total_ref[rows, cut] = total_in_ref[rows, cut] + value

    scale = time_step / power
    stencil(stack_in_ref, matrix_ref, moved_ref, "ab")
    advance("ab", old, keep, mixed_in_ref, moved_ref, pot_ref, drive, scale)
    mix(coupling_ref, stack_in_ref, now_ref, (2,))
    stencil(stack_in_ref, matrix_ref, moved_ref, "cd")
    mix(coupling_ref, stack_ref, mixed_ref, (0,))
    advance("cd", old, keep, now_ref, moved_ref, pot_ref, drive, scale)
    mix(coupling_ref, stack_in_ref, now_ref, (1,))
    advance(("ac", "bd"), old, keep, now_ref, moved_ref, pot_ref, drive, scale)
    mix(coupling_ref, stack_ref, mixed_ref, (2, 1))


def rest_kernel(
    first_ref,
    field_ref,
    after_ref,
    matrix_ref,
    coupling_ref,
    pot_ref,
    v_in_ref,
    stack_in_ref,
    mixed_in_ref,
    total_in_ref,
    out_any,
    v_ref,
    other_v_ref,
    stack_ref,
    other_stack_ref,
    mixed_ref,
    total_ref,
    moved_ref,
    sems,
):
    del after_ref
    local = 128
    radii = lane_radii(first_ref[0], local)
    drive = field_ref[1] * radii
    own_at = {OWN[part]: k for k, part in enumerate(PARTS)}
    vs, stacks = (v_ref, other_v_ref), (stack_ref, other_stack_ref)
    copies = [pltpu.make_async_copy(total_ref.at[k], out_any.at[k], sems.at[k]) for k in range(4)]
    for power in range(2, ORDER + 1):
        v, stack = vs[power % 2], stacks[power % 2]
        next_v, next_stack = vs[1 - power % 2], stacks[1 - power % 2]
        if power == 2:
            v, stack = v_in_ref, stack_in_ref
        mixed = mixed_in_ref if power == 2 else mixed_ref
        final = power == ORDER

        def old(at, rows):
            return v[rows, at : at + local]

        def keep(at, rows, value):
            cut = slice(at, at + local)
            if not final:
                next_v[rows, cut] = value
                split_rows(next_stack, at, rows, value)
            if at in own_at:
                k = own_at[at]
                before = total_in_ref[rows, cut] if power == 2 else total_ref[k, rows, :]
                total_ref[k, rows, :] = before + value

        scale = time_step / power
        for pair, tile in (("ab", 0), ("cd", 2)):
            if power > 2:
                mix(coupling_ref, stack, mixed_ref, (tile,))
            stencil(stack, matrix_ref, moved_ref, pair)
            advance(pair, old, keep, mixed, moved_ref, pot_ref, drive, scale)
            if final:
                for part in pair:
                    copies[PARTS.index(part)].start()
        if not final:
            if power > 2:
                mix(coupling_ref, stack, mixed_ref, (1,))
            advance(("ac", "bd"), old, keep, mixed, moved_ref, pot_ref, drive, scale)
    for copy in copies:
        copy.wait()


def tree(count):
    if count == 16:
        return [[2], [4, 8, 12]]
    return [[1 << k] for k in range(1, (count - 1).bit_length())]


def swaps(start, count):
    return [(start + i, 1 - 2 * (i % 2)) for i in range(count)]


def full_cycle(pairs, count):
    to = {i: i ^ 1 for i in range(count)}
    for a, b in pairs:
        to[a], to[b], to[b ^ 1], to[a ^ 1] = b, b ^ 1, a ^ 1, a
    return sorted(to.items())


def vmem(count):
    return [pl.BlockSpec(memory_space=pltpu.VMEM)] * count


def smem(count):
    return [pl.BlockSpec(memory_space=pltpu.SMEM)] * count


def params():
    return pltpu.CompilerParams(vmem_limit_bytes=32 * 1024 * 1024)


def per_device(states, dipole, pattern, angular, thresholds, surface_profile, pulse_field, *, count):
    channels, local = states.shape[1:]
    grid_points = local * count
    half = channels // 2
    axis = "radius"
    here = lax.axis_index(axis)
    first = (here * local).reshape(1).astype(jnp.int32)
    shape = jax.ShapeDtypeStruct
    width = 6 * local
    scaling = 1.0 / (math.sqrt(channels * grid_points) * (inner_radius + grid_points * spacing))

    near, far, inner = pl.pallas_call(
        pack_kernel,
        out_shape=(
            shape((half + 8, local), F32),
            shape((half + 8, local), F32),
            shape((half + 40, local), F32),
        ),
        in_specs=smem(1) + [pl.BlockSpec(memory_space=pltpu.HBM)] * 2,
        out_specs=tuple(vmem(3)),
        scratch_shapes=[
            pltpu.VMEM(states.shape, F32),
            pltpu.VMEM(surface_profile.shape, F32),
            pltpu.SemaphoreType.DMA((5,)),
        ],
        compiler_params=params(),
        name="pack",
    )(
        first,
        pltpu.with_memory_space_constraint(states, pltpu.HBM),
        pltpu.with_memory_space_constraint(surface_profile, pltpu.HBM),
    )

    coupling, kinetic, pot, stack, mixed, part = pl.pallas_call(
        functools.partial(table_kernel, grid_points=grid_points),
        out_shape=(
            shape((channels, 3 * channels), BF16),
            shape((2, 2 * local, 2 * local), F32),
            shape((channels, 2 * local), F32),
            shape((3 * channels, width), BF16),
            shape((channels, width), F32),
            shape((8, local), F32),
        ),
        in_specs=smem(1) + vmem(5),
        out_specs=tuple(vmem(6)),
        compiler_params=params(),
        name="tables",
    )(first, dipole, pattern, angular.reshape(1, channels), thresholds.reshape(1, channels), states)

    far = lax.ppermute(far, axis, [(i, i + d) for i, d in swaps(1, count - 2)])
    have, far_waits = [0], True
    for offsets in tree(count):
        fresh, chosen = [], inner
        for offset in offsets:
            pairs = [(h, h + offset) for h in have if h + offset < count]
            got = lax.ppermute(inner, axis, full_cycle(pairs, count))
            to = [p[1] for p in pairs]
            hit = functools.reduce(jnp.logical_or, [here == t for t in to])
            chosen = jnp.where(hit, got, chosen)
            fresh += to
        if len(have) > 1 and far_waits:
            chosen, far = lax.optimization_barrier((chosen, far))
            far_waits = False
        inner = chosen
        have += fresh
    sent = jnp.concatenate([inner, near])
    got = lax.ppermute(sent, axis, [(i, i + d) for i, d in swaps(0, count)])

    moved = pltpu.VMEM((4, channels, 2 * local), F32)
    evolved = (
        shape((channels, width), F32),
        shape((3 * channels, width), BF16),
        shape((channels, width), F32),
        shape((channels, width), F32),
    )
    stack, mixed, total, matrix, part = pl.pallas_call(
        functools.partial(first_kernel, scaling=scaling),
        out_shape=evolved[1:] + (shape((2, 2 * local, 2 * local), BF16), shape((8, local), F32)),
        in_specs=smem(2) + vmem(11),
        out_specs=tuple(vmem(5)),
        scratch_shapes=[
            pltpu.VMEM((channels, width), F32),
            pltpu.VMEM((channels, width), F32),
            pltpu.VMEM((3 * channels, width), BF16),
            moved,
            pltpu.VMEM((2, 2 * local, 2 * local), F32),
        ],
        input_output_aliases={11: 0, 12: 1},
        compiler_params=params(),
        name="first",
    )(first, pulse_field, far, got, sent, surface_profile, states, coupling, kinetic, pot, part, stack, mixed)

    bits = (count - 1).bit_length()
    groups = [range(low, min(low + 2, bits)) for low in range(0, bits, 2)]

    def send(value, group):
        low = group[0]
        return [
            lax.ppermute(value, axis, [(i, i ^ (pattern << low)) for i in range(count)])
            for pattern in range(1, 1 << len(group))
        ]

    def add(value, got):
        if len(got) == 1:
            return value + got[0]
        return (value + got[0]) + (got[1] + got[2])

    got = send(part, groups[0])
    v, stack, mixed, total, part = pl.pallas_call(
        functools.partial(later_kernel, power=1),
        out_shape=evolved + (shape(part.shape, F32),),
        in_specs=smem(2) + vmem(8),
        out_specs=tuple(vmem(5)),
        scratch_shapes=[moved, pltpu.VMEM((channels, width), F32)],
        compiler_params=params(),
        name="later",
    )(first, pulse_field, part, matrix, coupling, pot, total, stack, mixed, total)
    part = add(part, got)
    for group in groups[1:-1]:
        part = add(part, send(part, group))
    got = send(part, groups[-1])
    final = pl.pallas_call(
        rest_kernel,
        out_shape=shape(states.shape, F32),
        in_specs=smem(2) + vmem(8),
        out_specs=pl.BlockSpec(memory_space=pltpu.HBM),
        scratch_shapes=[
            pltpu.VMEM((channels, width), F32),
            pltpu.VMEM((channels, width), F32),
            pltpu.VMEM((3 * channels, width), BF16),
            pltpu.VMEM((3 * channels, width), BF16),
            pltpu.VMEM((channels, width), F32),
            pltpu.VMEM(states.shape, F32),
            moved,
            pltpu.SemaphoreType.DMA((4,)),
        ],
        compiler_params=params(),
        name="rest",
    )(first, pulse_field, part, matrix, coupling, pot, v, stack, mixed, total)
    part = add(part, got)
    return final, part[0, :STEPS]


def solution(mesh):
    return jax.shard_map(
        functools.partial(per_device, count=mesh.shape["radius"]),
        mesh=mesh,
        in_specs=(P("groups", None, "radius"), P(), P(), P(), P(), P(None, "radius"), P("groups")),
        out_specs=(P("groups", None, "radius"), P("groups")),
        check_vma=False,
    )
```

```python
import functools
import math

import jax
import jax.numpy as jnp
from jax import lax
from jax.experimental import pallas as pl
from jax.experimental.pallas import tpu as pltpu
from jax.sharding import PartitionSpec as P

STEPS = 2
ORDER = 4

inner_radius = 20.0
spacing = 0.08
time_step = 0.005

HALO = 2 * ORDER * STEPS
INNER = 2 * ORDER * STEPS + 2
KIN = 1.0 / (24.0 * spacing * spacing)
VALUE = (4.0, -6.0, 4.0, -1.0)
SLOPE = (-13.0 / 3.0, 9.5, -7.0, 11.0 / 6.0)

F32 = jnp.float32
BF16 = jnp.bfloat16

OWN = {"a": 0, "b": 128, "c": 512, "d": 640}
EXTRA = {"a": 256, "c": 256, "b": 384, "d": 384}
PARTS = ("a", "b", "c", "d")


def iota(shape, dim):
    return lax.broadcasted_iota(jnp.int32, shape, dim)


def is_odd(first, local):
    return lax.rem(lax.div(first, local), 2) == 1


def pack_kernel(first_ref, states_any, profile_any, near_ref, far_ref, inner_ref, states_ref, profile_ref, sems):
    channels = states_ref.shape[1]
    half = channels // 2
    local = states_ref.shape[2]
    copies = [pltpu.make_async_copy(states_any.at[k], states_ref.at[k], sems.at[k]) for k in range(4)]
    copies.append(pltpu.make_async_copy(profile_any, profile_ref, sems.at[4]))
    for copy in copies:
        copy.start()
    copies[4].wait()
    odd = is_odd(first_ref[0], local)
    zeros = jnp.zeros((6, local), F32)
    prof = profile_ref[...]
    turned = pltpu.roll(prof, HALO, 1)
    for ref, value in (
        (near_ref, jnp.where(odd, prof, turned)),
        (far_ref, jnp.where(odd, turned, prof)),
        (inner_ref, prof),
    ):
        ref[half : half + 2, :] = value
        ref[half + 2 : half + 8, :] = zeros
    group = iota((half, local), 1) // HALO
    groups = local // HALO
    right = left = None
    rest = [None, None]
    for k, first in ((0, 0), (2, 64), (1, 16), (3, 80)):
        copies[k].wait()
        for h in range(2):
            at = first + 32 * h
            moved = pltpu.roll(states_ref[k, half * h : half * h + half, :], (at + HALO) % local, 1)

            def put(old, to):
                return moved if old is None else jnp.where(group == to // HALO % groups, moved, old)

            right = put(right, at)
            left = put(left, at + HALO)
            rest[h] = put(rest[h], at + 2 * HALO)
    near_ref[:half, :] = jnp.where(odd, left, right)
    far_ref[:half, :] = jnp.where(odd, right, left)
    inner_ref[:half, :] = left
    lanes = iota((32, local), 1)
    more = None
    for h in range(2):
        for i in range((half + 31) // 32):
            rows = rest[h][32 * i : min(32 * i + 32, half)]
            if rows.shape[0] < 32:
                rows = jnp.concatenate([rows, jnp.zeros((32 - rows.shape[0], local), F32)], axis=0)
            moved = pltpu.roll(rows, 2 * i, 1) if i else rows
            hit = ((lanes & 15) // 2 == i) & ((lanes & 32) == 32 * (1 - h))
            more = moved if more is None else jnp.where(hit, moved, more)
    inner_ref[half + 8 :, :] = more


def lane_points(lanes, first, local):
    e = (lanes - local) & 63
    own = lanes < local
    point = jnp.where(
        own,
        first + lanes,
        jnp.where(
            e < 16,
            first - 16 + e,
            jnp.where(
                e < 32,
                first + local + e - 16,
                jnp.where(e < 32 + INNER, e - 32, e - 32 - INNER),
            ),
        ),
    )
    segment = jnp.where(
        own, 0, jnp.where(e < 32, 0, jnp.where(e < 32 + INNER, 1, jnp.where(e < 36 + INNER, 2, 3)))
    )
    return point, segment


def lane_radii(first, local):
    lanes = iota((8, 2 * local), 1)
    point, _ = lane_points(lanes, first, local)
    return (inner_radius + (point + 1).astype(F32) * spacing)[:1]


def table_kernel(
    first_ref,
    dipole_ref,
    pattern_ref,
    angular_ref,
    thr_ref,
    states_ref,
    coupling_ref,
    kinetic_ref,
    pot_ref,
    stack_ref,
    mixed_ref,
    part_ref,
    *,
    grid_points,
):
    channels = dipole_ref.shape[0]
    blocks = pattern_ref.shape[0]
    size = channels // blocks
    local = 128
    first = first_ref[0]
    pattern = pattern_ref[...].astype(F32)
    joined = jnp.maximum(pattern, pattern.T).astype(BF16)
    tall = (iota((channels, blocks), 0) // size == iota((channels, blocks), 1)).astype(F32).astype(BF16)
    wide = (iota((blocks, channels), 1) // size == iota((blocks, channels), 0)).astype(F32).astype(BF16)
    rows = jnp.dot(tall, joined, preferred_element_type=F32).astype(BF16)
    mask = jnp.dot(rows, wide, preferred_element_type=F32)
    ang = jnp.broadcast_to(angular_ref[...].astype(F32), (channels, channels))
    angt = ang.T
    allowed = (mask > 0.5) & (jnp.abs(ang - angt) == 1.0)
    dip = dipole_ref[...]
    coupling = jnp.where(allowed, 0.5 * (dip + dip.T), 0.0)
    high = coupling.astype(BF16)
    low = (coupling - high.astype(F32)).astype(BF16)
    coupling_ref[...] = jnp.concatenate([high, high, low], axis=1)
    radii = lane_radii(first, local)
    inverse = 1.0 / (radii * radii)
    centrifugal = 0.5 * angt[:, :local] * (angt[:, :local] + 1.0)
    thr = jnp.broadcast_to(thr_ref[...], (local, channels)).T
    pot_ref[:, :local] = thr + centrifugal * inverse[:, :local]
    pot_ref[:, local:] = thr + centrifugal * inverse[:, local:]
    shape = (2 * local, 2 * local)
    src, dst = iota(shape, 0), iota(shape, 1)
    sp, ss = lane_points(src, first, local)
    dp, ds = lane_points(dst, first, local)
    gap = jnp.abs(sp - dp)
    coef = jnp.where(gap == 0, 30.0, jnp.where(gap == 1, -16.0, jnp.where(gap == 2, 1.0, 0.0)))
    same = (ss < 2) & (ss == jnp.minimum(ds, 1))
    valid = (dp >= 0) & (dp < grid_points) & (ds < 3)
    coef = jnp.where(same & valid, coef, 0.0)
    for which in range(2):
        mine = (src < local) | ((src - local) // 64 == which)
        mine = mine & ((dst < local) | ((dst - local) // 64 == which))
        kinetic_ref[which] = jnp.where(mine, coef, 0.0)
    for k, part in enumerate(PARTS):
        split_store(stack_ref, OWN[part], states_ref[k])
    mix(coupling_ref, stack_ref, mixed_ref, (0, 2))
    part_ref[0:1, :] = intersect(states_ref[2], states_ref[3], mixed_ref, radii)
    part_ref[1:, :] = jnp.zeros((part_ref.shape[0] - 1, local), F32)


def split_store(stack_ref, at, value):
    channels = value.shape[0]
    width = value.shape[1]
    high = value.astype(BF16)
    low = (value - high.astype(F32)).astype(BF16)
    stack_ref[:channels, at : at + width] = high
    stack_ref[channels : 2 * channels, at : at + width] = low
    stack_ref[2 * channels :, at : at + width] = high


def mix(coupling_ref, stack_ref, mixed_ref, tiles):
    for n in tiles:
        cut = slice(256 * n, 256 * n + 256)
        mixed_ref[:, cut] = jnp.dot(coupling_ref[...], stack_ref[:, cut], preferred_element_type=F32)


def stencil(stack_ref, matrix_ref, moved_ref, parts):
    channels = stack_ref.shape[0] // 3
    for part in parts:
        own, extra = OWN[part], EXTRA[part]
        weights = matrix_ref[0 if part in "ab" else 1]
        left = [
            stack_ref[rows, at : at + 128]
            for rows in (slice(0, channels), slice(channels, 2 * channels))
            for at in (own, extra)
        ]
        moved_ref[PARTS.index(part)] = jnp.dot(jnp.concatenate(left, axis=1), weights, preferred_element_type=F32)


def advance(targets, old, keep, mixed_ref, moved_ref, pot_ref, drive, scale, chunk=80):
    channels, local = pot_ref.shape[0], 128
    own, extra = slice(0, local), slice(local, 2 * local)
    for c0 in range(0, channels, chunk):
        rows = slice(c0, c0 + chunk)
        for target in targets:
            sign = 1.0 if target in ("a", "c", "ac") else -1.0
            if len(target) == 1:
                source = {"a": "b", "b": "a", "c": "d", "d": "c"}[target]
                to, at, lanes = OWN[target], OWN[source], own
                moved = moved_ref[PARTS.index(source), rows, own]
            else:
                k, m = (1, 3) if target == "ac" else (0, 2)
                to, at, lanes = EXTRA[target[0]], EXTRA[PARTS[k]], extra
                moved = moved_ref[k, rows, extra] + moved_ref[m, rows, extra]
            factor = sign * scale
            value = (
                (factor * KIN) * moved
                + (factor * pot_ref[rows, lanes]) * old(at, rows)
                + (factor * drive[:, lanes]) * mixed_ref[rows, at : at + local]
            )
            keep(to, rows, value)


def split_rows(stack_ref, at, rows, value):
    channels = stack_ref.shape[0] // 3
    high = value.astype(BF16)
    low = (value - high.astype(F32)).astype(BF16)
    cut = slice(at, at + value.shape[1])
    stack_ref[rows, cut] = high
    stack_ref[channels + rows.start : channels + rows.stop, cut] = low
    stack_ref[2 * channels + rows.start : 2 * channels + rows.stop, cut] = high


def intersect(third, fourth, mixed_ref, radii):
    def mixed(part):
        return mixed_ref[:, OWN[part] : OWN[part] + 128]

    both = third * mixed("b") - fourth * mixed("a")
    return jnp.sum(both * radii[:, :128], axis=0, keepdims=True)


def first_kernel(
    first_ref,
    field_ref,
    far_ref,
    got_ref,
    sent_ref,
    profile_ref,
    states_ref,
    coupling_ref,
    kinetic_ref,
    pot_ref,
    part_in_ref,
    stack_in_ref,
    mixed_in_ref,
    stack_ref,
    mixed_ref,
    state_ref,
    matrix_ref,
    part_ref,
    v_ref,
    other_v_ref,
    other_stack_ref,
    moved_ref,
    work_ref,
    *,
    scaling,
):
    del stack_in_ref, mixed_in_ref
    channels = v_ref.shape[0]
    half = channels // 2
    local = 128
    first = first_ref[0]
    odd = is_odd(first, local)
    split = half + 40
    inner = jnp.where(odd, got_ref[:split, :], sent_ref[:split, :])
    left = jnp.where(odd, got_ref[split:, :], far_ref[...])
    right = jnp.where(odd, far_ref[...], got_ref[split:, :])
    lanes = iota((half, local), 1) & 63
    for pair, at in ((0, 256), (1, 384)):
        for h in range(2):
            back = 16 * pair + 32 * h

            def rolled(value, to):
                shift = (to - back) % local
                return pltpu.roll(value, shift, 1) if shift else value

            halo = jnp.where(((lanes - back) & 63) < 16, left[:half, :], right[:half, :])
            value = jnp.where(
                lanes < 32,
                rolled(halo, 0),
                jnp.where(
                    lanes < 48,
                    rolled(inner[:half, :], 16),
                    jnp.where((lanes >= 50) & (lanes < 54), rolled(inner[:half, :], 34), 0.0),
                ),
            )
            v_ref[half * h : half * h + half, at : at + local] = value
            narrow = iota((32, local), 1) & 63
            for i in range((half + 31) // 32):
                rows = slice(half * h + 32 * i, half * h + min(32 * i + 32, half))
                count = rows.stop - rows.start
                value = rolled(inner[half + 8 : half + 8 + count, :], 16 - 2 * i)
                hit = (narrow[:count] >= 48) & (narrow[:count] < 50)
                v_ref[rows, at : at + local] = jnp.where(hit, value, v_ref[rows, at : at + local])
    split_store(stack_ref, 256, v_ref[:, 256:512])
    p_own = profile_ref[...]
    lanes2 = iota((2, local), 1)
    inner_profile = inner[half : half + 2, :]
    p_extra = jnp.where(
        lanes2 < 16,
        left[half : half + 2, :],
        jnp.where(
            lanes2 < 32,
            pltpu.roll(right[half : half + 2, :], 16, 1),
            jnp.where(
                lanes2 < 32 + INNER,
                pltpu.roll(inner_profile, 32, 1),
                jnp.where(lanes2 < 36 + INNER, pltpu.roll(inner_profile, 32 + INNER, 1), 0.0),
            ),
        ),
    )
    p_extra = jnp.where(lanes2 < 64, p_extra, pltpu.roll(p_extra, 64, 1))
    profile = jnp.concatenate([p_own, p_extra], axis=1)
    cols = iota((1, 2 * local), 1)
    work_ref[...] = kinetic_ref[...]
    for which in range(2):
        mine = (cols < local) | ((cols - local) // 64 == which)
        for i in range(4):
            row = (VALUE[i] / KIN) * profile[0:1] + (SLOPE[i] / KIN) * profile[1:2]
            at = local + 64 * which + 32 + i
            row = jnp.where(mine, row, 0.0) + work_ref[which, at : at + 1, :]
            high = row.astype(BF16).astype(F32)
            work_ref[which, at : at + 1, :] = high
            at = local + 64 * which + 32 + INNER + i
            work_ref[which, at : at + 1, :] = row - high
    matrix_ref[:, : 2 * local, :] = work_ref[...].astype(BF16)
    matrix_ref[:, 2 * local :, :] = work_ref[...].astype(BF16)
    radii = lane_radii(first, local)
    drive = field_ref[0] * radii
    own_at = {OWN[part]: k for k, part in enumerate(PARTS)}
    vs, stacks = (v_ref, other_v_ref), (stack_ref, other_stack_ref)
    for power in range(1, ORDER + 1):
        v, stack = vs[1 - power % 2], stacks[1 - power % 2]
        next_v, next_stack = vs[power % 2], stacks[power % 2]

        def old(at, rows):
            if power == 1 and at in own_at:
                return states_ref[own_at[at], rows, :]
            return v[rows, at : at + local]

        def keep(at, rows, value):
            cut = slice(at, at + local)
            before = old(at, rows) if power == 1 else state_ref[rows, cut]
            state_ref[rows, cut] = before + value
            if power < ORDER:
                next_v[rows, cut] = value
                split_rows(next_stack, at, rows, value)
            else:
                split_rows(next_stack, at, rows, before + value)

        scale = time_step / power
        for pair, tile in (("ab", 0), ("cd", 2)):
            if power > 1:
                mix(coupling_ref, stack, mixed_ref, (tile,))
            stencil(stack, matrix_ref, moved_ref, pair)
            advance(pair, old, keep, mixed_ref, moved_ref, pot_ref, drive, scale)
        mix(coupling_ref, stack, mixed_ref, (1,))
        if power == ORDER:
            mix(coupling_ref, stack_ref, mixed_ref, (0,))
        advance(("ac", "bd"), old, keep, mixed_ref, moved_ref, pot_ref, drive, scale)
    part_ref[...] = jnp.zeros(part_ref.shape, F32)
    state = [state_ref[:, OWN[part] : OWN[part] + local] for part in "cd"]
    for n, value in ((0, part_in_ref[0:1, :]), (1, intersect(state[0], state[1], mixed_ref, radii))):
        whole = jnp.sum(value, axis=1, keepdims=True) * scaling
        here = (iota(part_ref.shape, 0) == 0) & (iota(part_ref.shape, 1) == n)
        part_ref[...] = jnp.where(here, whole, part_ref[...])


def later_kernel(
    first_ref,
    field_ref,
    after_ref,
    matrix_ref,
    coupling_ref,
    pot_ref,
    v_in_ref,
    stack_in_ref,
    mixed_in_ref,
    total_in_ref,
    v_ref,
    stack_ref,
    mixed_ref,
    total_ref,
    kept_ref,
    moved_ref,
    now_ref,
    *,
    power,
):
    kept_ref[...] = after_ref[...]
    local = 128
    radii = lane_radii(first_ref[0], local)
    drive = field_ref[1] * radii

    def old(at, rows):
        return v_in_ref[rows, at : at + local]

    def keep(at, rows, value):
        cut = slice(at, at + local)
        v_ref[rows, cut] = value
        split_rows(stack_ref, at, rows, value)
        if at in OWN.values():
            total_ref[rows, cut] = total_in_ref[rows, cut] + value

    scale = time_step / power
    stencil(stack_in_ref, matrix_ref, moved_ref, "ab")
    advance("ab", old, keep, mixed_in_ref, moved_ref, pot_ref, drive, scale)
    mix(coupling_ref, stack_in_ref, now_ref, (2,))
    stencil(stack_in_ref, matrix_ref, moved_ref, "cd")
    mix(coupling_ref, stack_ref, mixed_ref, (0,))
    advance("cd", old, keep, now_ref, moved_ref, pot_ref, drive, scale)
    mix(coupling_ref, stack_in_ref, now_ref, (1,))
    advance(("ac", "bd"), old, keep, now_ref, moved_ref, pot_ref, drive, scale)
    mix(coupling_ref, stack_ref, mixed_ref, (2, 1))


def rest_kernel(
    first_ref,
    field_ref,
    after_ref,
    matrix_ref,
    coupling_ref,
    pot_ref,
    v_in_ref,
    stack_in_ref,
    mixed_in_ref,
    total_in_ref,
    out_any,
    v_ref,
    other_v_ref,
    stack_ref,
    other_stack_ref,
    mixed_ref,
    total_ref,
    moved_ref,
    sems,
):
    del after_ref
    local = 128
    radii = lane_radii(first_ref[0], local)
    drive = field_ref[1] * radii
    own_at = {OWN[part]: k for k, part in enumerate(PARTS)}
    vs, stacks = (v_ref, other_v_ref), (stack_ref, other_stack_ref)
    copies = [pltpu.make_async_copy(total_ref.at[k], out_any.at[k], sems.at[k]) for k in range(4)]
    for power in range(2, ORDER + 1):
        v, stack = vs[power % 2], stacks[power % 2]
        next_v, next_stack = vs[1 - power % 2], stacks[1 - power % 2]
        if power == 2:
            v, stack = v_in_ref, stack_in_ref
        mixed = mixed_in_ref if power == 2 else mixed_ref
        final = power == ORDER

        def old(at, rows):
            return v[rows, at : at + local]

        def keep(at, rows, value):
            cut = slice(at, at + local)
            if not final:
                next_v[rows, cut] = value
                split_rows(next_stack, at, rows, value)
            if at in own_at:
                k = own_at[at]
                before = total_in_ref[rows, cut] if power == 2 else total_ref[k, rows, :]
                total_ref[k, rows, :] = before + value

        scale = time_step / power
        for pair, tile in (("ab", 0), ("cd", 2)):
            if power > 2:
                mix(coupling_ref, stack, mixed_ref, (tile,))
            stencil(stack, matrix_ref, moved_ref, pair)
            advance(pair, old, keep, mixed, moved_ref, pot_ref, drive, scale)
            if final:
                for part in pair:
                    copies[PARTS.index(part)].start()
        if not final:
            if power > 2:
                mix(coupling_ref, stack, mixed_ref, (1,))
            advance(("ac", "bd"), old, keep, mixed, moved_ref, pot_ref, drive, scale)
    for copy in copies:
        copy.wait()


def tree(count):
    if count == 16:
        return [[2], [4, 8, 12]]
    return [[1 << k] for k in range(1, (count - 1).bit_length())]


def swaps(start, count):
    return [(start + i, 1 - 2 * (i % 2)) for i in range(count)]


def full_cycle(pairs, count):
    to = {i: i ^ 1 for i in range(count)}
    for a, b in pairs:
        to[a], to[b], to[b ^ 1], to[a ^ 1] = b, b ^ 1, a ^ 1, a
    return sorted(to.items())


def vmem(count):
    return [pl.BlockSpec(memory_space=pltpu.VMEM)] * count


def smem(count):
    return [pl.BlockSpec(memory_space=pltpu.SMEM)] * count


def params():
    return pltpu.CompilerParams(vmem_limit_bytes=32 * 1024 * 1024)


def per_device(states, dipole, pattern, angular, thresholds, surface_profile, pulse_field, *, count):
    channels, local = states.shape[1:]
    grid_points = local * count
    half = channels // 2
    axis = "radius"
    here = lax.axis_index(axis)
    first = (here * local).reshape(1).astype(jnp.int32)
    shape = jax.ShapeDtypeStruct
    width = 6 * local
    scaling = 1.0 / (math.sqrt(channels * grid_points) * (inner_radius + grid_points * spacing))

    near, far, inner, own = pl.pallas_call(
        pack_kernel,
        out_shape=(
            shape((half + 8, local), F32),
            shape((half + 8, local), F32),
            shape((half + 40, local), F32),
            shape(states.shape, F32),
        ),
        in_specs=smem(1) + [pl.BlockSpec(memory_space=pltpu.HBM)] * 2,
        out_specs=tuple(vmem(4)),
        scratch_shapes=[
            pltpu.VMEM(surface_profile.shape, F32),
            pltpu.SemaphoreType.DMA((5,)),
        ],
        compiler_params=params(),
        name="pack",
    )(
        first,
        pltpu.with_memory_space_constraint(states, pltpu.HBM),
        pltpu.with_memory_space_constraint(surface_profile, pltpu.HBM),
    )

    coupling, kinetic, pot, stack, mixed, part = pl.pallas_call(
        functools.partial(table_kernel, grid_points=grid_points),
        out_shape=(
            shape((channels, 3 * channels), BF16),
            shape((2, 2 * local, 2 * local), F32),
            shape((channels, 2 * local), F32),
            shape((3 * channels, width), BF16),
            shape((channels, width), F32),
            shape((8, local), F32),
        ),
        in_specs=smem(1) + vmem(5),
        out_specs=tuple(vmem(6)),
        compiler_params=params(),
        name="tables",
    )(first, dipole, pattern, angular.reshape(1, channels), thresholds.reshape(1, channels), own)

    far = lax.ppermute(far, axis, [(i, i + d) for i, d in swaps(1, count - 2)])
    have, far_waits = [0], True
    for offsets in tree(count):
        fresh, chosen = [], inner
        for offset in offsets:
            pairs = [(h, h + offset) for h in have if h + offset < count]
            got = lax.ppermute(inner, axis, full_cycle(pairs, count))
            to = [p[1] for p in pairs]
            hit = functools.reduce(jnp.logical_or, [here == t for t in to])
            chosen = jnp.where(hit, got, chosen)
            fresh += to
        if len(have) > 1 and far_waits:
            chosen, far = lax.optimization_barrier((chosen, far))
            far_waits = False
        inner = chosen
        have += fresh
    sent = jnp.concatenate([inner, near])
    got = lax.ppermute(sent, axis, [(i, i + d) for i, d in swaps(0, count)])

    moved = pltpu.VMEM((4, channels, 2 * local), F32)
    evolved = (
        shape((channels, width), F32),
        shape((3 * channels, width), BF16),
        shape((channels, width), F32),
        shape((channels, width), F32),
    )
    stack, mixed, total, matrix, part = pl.pallas_call(
        functools.partial(first_kernel, scaling=scaling),
        out_shape=evolved[1:] + (shape((2, 4 * local, 2 * local), BF16), shape((8, local), F32)),
        in_specs=smem(2) + vmem(11),
        out_specs=tuple(vmem(5)),
        scratch_shapes=[
            pltpu.VMEM((channels, width), F32),
            pltpu.VMEM((channels, width), F32),
            pltpu.VMEM((3 * channels, width), BF16),
            moved,
            pltpu.VMEM((2, 2 * local, 2 * local), F32),
        ],
        input_output_aliases={11: 0, 12: 1},
        compiler_params=params(),
        name="first",
    )(first, pulse_field, far, got, sent, surface_profile, own, coupling, kinetic, pot, part, stack, mixed)

    bits = (count - 1).bit_length()
    groups = [range(low, min(low + 2, bits)) for low in range(0, bits, 2)]

    def send(value, group):
        low = group[0]
        return [
            lax.ppermute(value, axis, [(i, i ^ (pattern << low)) for i in range(count)])
            for pattern in range(1, 1 << len(group))
        ]

    def add(value, got):
        if len(got) == 1:
            return value + got[0]
        return (value + got[0]) + (got[1] + got[2])

    got = send(part, groups[0])
    v, stack, mixed, total, part = pl.pallas_call(
        functools.partial(later_kernel, power=1),
        out_shape=evolved + (shape(part.shape, F32),),
        in_specs=smem(2) + vmem(8),
        out_specs=tuple(vmem(5)),
        scratch_shapes=[moved, pltpu.VMEM((channels, width), F32)],
        compiler_params=params(),
        name="later",
    )(first, pulse_field, part, matrix, coupling, pot, total, stack, mixed, total)
    part = add(part, got)
    for group in groups[1:-1]:
        part = add(part, send(part, group))
    got = send(part, groups[-1])
    final = pl.pallas_call(
        rest_kernel,
        out_shape=shape(states.shape, F32),
        in_specs=smem(2) + vmem(8),
        out_specs=pl.BlockSpec(memory_space=pltpu.HBM),
        scratch_shapes=[
            pltpu.VMEM((channels, width), F32),
            pltpu.VMEM((channels, width), F32),
            pltpu.VMEM((3 * channels, width), BF16),
            pltpu.VMEM((3 * channels, width), BF16),
            pltpu.VMEM((channels, width), F32),
            pltpu.VMEM(states.shape, F32),
            moved,
            pltpu.SemaphoreType.DMA((4,)),
        ],
        compiler_params=params(),
        name="rest",
    )(first, pulse_field, part, matrix, coupling, pot, v, stack, mixed, total)
    part = add(part, got)
    return final, part[0, :STEPS]


def solution(mesh):
    return jax.shard_map(
        functools.partial(per_device, count=mesh.shape["radius"]),
        mesh=mesh,
        in_specs=(P("groups", None, "radius"), P(), P(), P(), P(), P(None, "radius"), P("groups")),
        out_specs=(P("groups", None, "radius"), P("groups")),
        check_vma=False,
    )
```
